32 devices in a mesh: dp: 8 (over y, x, core), replica: 4 (over z).
Axes of the slice: x: 2, y: 2, z: 4, core: 2. Of those that a mesh axis runs over, the one named last changes fastest.
Arguments:
- gradient: bfloat16 [4, 8, 8, 8192], P('replica', 'dp'), may hold values from -6 to 6
- master: float32 [8, 8192], P('dp', 'replica'), may hold values from -0.0625 to 0.0625
- moment: float32 [8, 8192], P('dp', 'replica'), may hold values from -0.046875 to 0.046875
- second: float32 [8, 8192], P('dp', 'replica'), may hold values from 1e-06 to 0.0001
Outputs:
- new_params: bfloat16 [8, 8192], P('dp')
- new_master: float32 [8, 8192], P('dp', 'replica')
- new_moment: float32 [8, 8192], P('dp', 'replica')
- new_second: float32 [8, 8192], P('dp', 'replica')
- direction: float32 [8, 8192], P('dp', 'replica')
- ratios: float32 [4], replicated
The draws below stay inside these ranges and needn't reach their ends.
All inputs are finite; a program needn't handle non-finite values.
Results may differ from the reference program's by a relative error of at most 0.001.
Values may be sent and summed in bfloat16 or wider, within the bound.
A program may use at most 64 MiB of HBM per device.

```python
import math
import jax
import jax.numpy as jnp
from jax import lax

D = 8192
MATS = 4
STEP = 2
ROWS = 8
N_DP = 8
N_REPLICA = 4


def with_spikes(array, rng, source, target, parts, factor):
    def block_of(dim):
        return (jnp.arange(array.shape[dim]) // (array.shape[dim] // parts)).reshape((-1,) + (1,) * (array.ndim - 1 - dim))

    first = jax.random.permutation(rng, parts)[block_of(target)]
    far = (block_of(target) + parts // 2) % parts
    return jnp.where((block_of(source) == first) | (block_of(source) == far), factor * array, array)


def block_levels(stream_key, shape, split, low, high):
    loudness, own = 1.0, jax.random.fold_in(stream_key, 6)
    for position, parts in split:
        draws = jnp.exp(jax.random.uniform(jax.random.fold_in(own, position), (parts,), jnp.float32, low / len(split), high / len(split)))
        loudness = loudness * jnp.repeat(draws, shape[position] // parts).reshape([-1 if axis == position else 1 for axis in range(len(shape))])
    return loudness


def noise(own_key, dims, width, limit, cuts=(), kind=jnp.bfloat16):
    result = jax.random.normal(own_key, dims, jnp.float32) * width
    if len(cuts) > 0:
        result = block_levels(own_key, dims, cuts, -0.22, 0.18) * result
    return jnp.clip(result, min=-limit, max=limit).astype(kind)


def heavy_noise(stream_key, dims, deviation, reach, pieces, heavy, held_as=jnp.bfloat16):
    values = deviation * jax.random.normal(stream_key, dims, jnp.float32)
    if pieces:
        values = values * block_levels(stream_key, dims, pieces, -0.22, 0.18)
    return jnp.clip(with_spikes(values, jax.random.fold_in(stream_key, 3), *heavy), -reach, reach).astype(held_as)


def setup_inputs(seed: int = 0) -> dict:
    key_list = jax.random.split(jax.random.key(seed), 5)
    gradient = heavy_noise(key_list[0], (N_REPLICA, N_DP, ROWS, D), 1.0, 6.0, ((0, 4), (1, 8)), (1, 2, 8, 2.0))
    master = noise(key_list[1], (ROWS, D), D ** -0.5, 0.0625, ((0, 8), (1, 4)), jnp.float32)
    moment = noise(key_list[2], (ROWS, D), 0.003, 0.046875, ((0, 8), (1, 4)), jnp.float32)
    second = jnp.clip(jnp.exp(math.log(0.0001) - 4.6051702 * jax.random.uniform(key_list[3], (ROWS, D), jnp.float32) ** block_levels(key_list[3], (ROWS, D), ((0, 8), (1, 4)), -0.2, 0.2)), 9.999999974752427e-07, 0.0001)
    return dict(gradient=gradient, master=master, moment=moment, second=second)


def reference(gradient, master, moment, second):

    def add_block(total, block):
        return (total + lax.optimization_barrier(jnp.sum(block.astype(jnp.float32), axis=0)), None)
    start = jnp.zeros((ROWS, D), jnp.float32)
    total, unused = lax.scan(add_block, start, gradient)
    grad = total / (N_REPLICA * N_DP)
    new_moment = 0.9 * moment + 0.1 * grad
    new_second = 0.999 * second + 0.001 * grad * grad
    first_fix = 1.0 - 0.9 ** STEP
    second_fix = 1.0 - 0.999 ** STEP
    direction = new_moment / first_fix / (jnp.sqrt(new_second / second_fix) + 1e-08)
    new_master = master - 0.0003 * (direction + 0.1 * master)
    new_params = new_master.astype(jnp.bfloat16)
    dir_sq = lax.optimization_barrier(jnp.sum((direction * direction).reshape(MATS, ROWS // MATS * D), axis=1))
    wgt_sq = lax.optimization_barrier(jnp.sum((master * master).reshape(MATS, ROWS // MATS * D), axis=1))
    ratios = jnp.sqrt(dir_sq) / (jnp.sqrt(wgt_sq) + 1e-06)
    return (new_params, new_master, new_moment, new_second, direction, ratios)
```

```python
import functools

import jax
import jax.numpy as jnp
from jax import lax
from jax.experimental import pallas as pl
from jax.experimental.pallas import tpu as pltpu
from jax.sharding import PartitionSpec as P

MATS = 4
STEP = 2
LANES = 128
IDS = pl.DeviceIdType.MESH
FIRST_SCALE = 1.0 / (1.0 - 0.9**STEP)
SECOND_SCALE = 1.0 / (1.0 - 0.999**STEP)
OWNERS = ((1, 0), (3, 0), (1, 1), (3, 1), (5, 1), (1, 2), (3, 2), (5, 2))
DIRECT_BYTES = 16 * 2**20


def adam(grad, master, moment, second):
    new_moment = 0.9 * moment + 0.1 * grad
    new_second = 0.999 * second + 0.001 * grad * grad
    direction = new_moment * FIRST_SCALE / (jnp.sqrt(new_second * SECOND_SCALE) + 1e-08)
    new_master = master - 0.0003 * (direction + 0.1 * master)
    return new_master, new_moment, new_second, direction


def direct_kernel(n_dp, n_rep, grad_hbm, master_hbm, moment_hbm, second_hbm,
                  row_out, blocks_out, ratio_out,
                  mine, raw_in, state_in, tiles, grad_out, grad_in, msg_out, msg_in,
                  load_sem, raw_send, raw_recv, state_send, state_recv,
                  grad_send, grad_recv, msg_send, msg_recv):
    dp = lax.axis_index("dp")
    rep = lax.axis_index("replica")
    n_own = len(OWNERS)
    per = n_own // n_rep
    rows, width = grad_hbm.shape
    wide = width // n_own
    block = wide // LANES
    f32 = jnp.float32

    def settle(ref, sem):
        pltpu.make_async_copy(ref, ref, sem).wait()

    def remote(src, dst, send, recv, device):
        return pltpu.make_async_remote_copy(
            src_ref=src, dst_ref=dst, send_sem=send, recv_sem=recv,
            device_id=device, device_id_type=IDS)

    def copy_to(here, src, dst, send, recv, device):
        @pl.when(here)
        def _():
            pltpu.make_async_copy(src, dst, recv).start()

        @pl.when(jnp.logical_not(here))
        def _():
            remote(src, dst, send, recv, device).start()

    is_me = [(dp == d) & (rep == r) for d, r in OWNERS]
    owner = functools.reduce(jnp.logical_or, is_me)
    index = sum(b * m.astype(jnp.int32) for b, m in enumerate(is_me))

    barrier = pltpu.get_barrier_semaphore()

    @pl.when(owner)
    def _():
        for k in range(n_dp):
            for r in range(n_rep):
                if k or r:
                    pl.semaphore_signal(
                        barrier, inc=1, device_id=(lax.rem(dp + k, n_dp), lax.rem(rep + r, n_rep)),
                        device_id_type=IDS)

    state_hbm = (master_hbm, moment_hbm, second_hbm)
    loads = [pltpu.make_async_copy(ref, mine.at[i], load_sem.at[i]) for i, ref in enumerate(state_hbm)]
    for load in loads:
        load.start()
    with jax.named_scope("enter"):
        pl.semaphore_wait(barrier, n_own - owner.astype(jnp.int32))

    slot = rep * n_dp + dp
    for b, device in enumerate(OWNERS):
        copy_to(is_me[b], grad_hbm.at[:, b * wide:(b + 1) * wide], raw_in.at[slot],
                raw_send.at[b], raw_recv.at[rep], device)
    for b, device in enumerate(OWNERS):
        @pl.when(rep == b // per)
        def _():
            sub = b % per
            for i, ref in enumerate(state_hbm):
                copy_to(is_me[b], ref.at[sub * block:(sub + 1) * block], state_in.at[i, dp],
                        state_send.at[sub], state_recv.at[0], device)

    @pl.when(owner)
    def _():
        total = None
        for z in (1, 0, *range(2, n_rep)):
            with jax.named_scope(f"wait_raw{z}"):
                settle(raw_in.at[z * n_dp:(z + 1) * n_dp], raw_recv.at[z])
            for s in range(z * n_dp, (z + 1) * n_dp):
                part = raw_in[s].astype(f32)
                total = part if total is None else total + part
        total = total * (1.0 / (n_dp * n_rep))
        for t in range(block):
            tiles[t * rows:(t + 1) * rows, :] = total[:, t * LANES:(t + 1) * LANES]
        for r in range(rows):
            grad_out[r] = tiles[pl.ds(r, block, stride=rows), :]
        place = index // per
        for r in range(rows):
            copy_to((dp == r) & (rep == place), grad_out.at[r], grad_in.at[lax.rem(index, per)],
                    grad_send.at[r], grad_recv.at[0], (r, place))
        with jax.named_scope("wait_state"):
            settle(state_in, state_recv.at[0])
        master = state_in[0]
        new_master, _, _, direction = adam(grad_out[...], master, state_in[1], state_in[2])
        sums = [jnp.sum(v * v, axis=1) for v in (direction, master)]
        per_mat = rows // MATS
        stats = jnp.concatenate(
            [jnp.sum(v[m * per_mat:(m + 1) * per_mat], axis=0, keepdims=True) for m in range(MATS) for v in sums],
            axis=0)
        for r in range(rows):
            msg_out[r, 0:block] = new_master[r]
            msg_out[r, block:] = stats
        for z in range(n_rep):
            for r in range(rows):
                copy_to((dp == r) & (rep == z), msg_out.at[r], msg_in.at[index],
                        msg_send.at[r], msg_recv.at[0], (r, z))

    for load in loads:
        load.wait()
    for b in range(n_own):
        @pl.when(jnp.logical_not(is_me[b]))
        def _():
            settle(raw_in.at[0], raw_send.at[b])

            @pl.when(rep == b // per)
            def _():
                settle(state_in.at[:, 0], state_send.at[b % per])

    with jax.named_scope("wait_grad"):
        settle(grad_in, grad_recv.at[0])
    grad = grad_in[...].reshape(per * block, LANES)
    for i, value in enumerate(adam(grad, mine[0], mine[1], mine[2])):
        blocks_out[i] = value
    with jax.named_scope("wait_msg"):
        settle(msg_in, msg_recv.at[0])
    for b in range(n_own):
        row_out[b * block:(b + 1) * block] = msg_in[b, 0:block]
    stats = msg_in[0, block:]
    for b in range(1, n_own):
        stats = stats + msg_in[b, block:]
    norms = jnp.sqrt(jnp.sum(stats, axis=1, keepdims=True))
    lane = lax.broadcasted_iota(jnp.int32, (1, LANES), 1)
    ratios = jnp.zeros((1, LANES), f32)
    for m in range(MATS):
        ratio = norms[2 * m:2 * m + 1] / (norms[2 * m + 1:2 * m + 2] + 1e-06)
        ratios = jnp.where(lane == m, ratio, ratios)
    ratio_out[...] = ratios

    @pl.when(owner)
    def _():
        place = index // per
        for r in range(rows):
            here = (dp == r) & (rep == place)

            @pl.when(jnp.logical_not(here))
            def _():
                settle(grad_out.at[r], grad_send.at[r])

            @pl.when(dp == r)
            def _():
                settle(msg_in.at[0:n_rep - 1], msg_send.at[r])

            @pl.when(dp != r)
            def _():
                settle(msg_in.at[0:n_rep], msg_send.at[r])


def direct(raw_rows, flat, n_dp, n_rep):
    rows, width = raw_rows.shape
    n_own = len(OWNERS)
    per = n_own // n_rep
    length, wide = width // LANES, width // n_own
    block = wide // LANES
    f32 = jnp.float32
    dma = pltpu.SemaphoreType.DMA
    return pl.pallas_call(
        functools.partial(direct_kernel, n_dp, n_rep),
        out_shape=[
            pltpu.VMEM((length, LANES), f32),
            pltpu.VMEM((4, per * block, LANES), f32),
            pltpu.VMEM((1, LANES), f32),
        ],
        in_specs=[pl.BlockSpec(memory_space=pl.ANY)] * 4,
        out_specs=[pl.BlockSpec(memory_space=pltpu.VMEM)] * 3,
        scratch_shapes=[
            pltpu.VMEM((3, per * block, LANES), f32),
            pltpu.VMEM((n_dp * n_rep, rows, wide), jnp.bfloat16),
            pltpu.VMEM((3, rows, block, LANES), f32),
            pltpu.VMEM((rows * block, LANES), f32),
            pltpu.VMEM((rows, block, LANES), f32),
            pltpu.VMEM((per, block, LANES), f32),
            pltpu.VMEM((rows, block + 2 * MATS, LANES), f32),
            pltpu.VMEM((n_own, block + 2 * MATS, LANES), f32),
            dma((3,)), dma((n_own,)), dma((n_rep,)), dma((per,)), dma((1,)),
            dma((rows,)), dma((1,)), dma((rows,)), dma((1,)),
        ],
        compiler_params=pltpu.CompilerParams(collective_id=0, has_side_effects=True),
    )(raw_rows, *flat)


def rows_kernel(n_dp, n_rep, grad_hbm, master_hbm, moment_hbm, second_hbm,
                row_out, blocks_out, ratio_out,
                raw, state, tiles, rows_out, rows_in, parts, full, stats,
                load_sem, state_send, state_recv, row_send, row_recv,
                part_send, part_recv, stat_send, stat_recv):
    dp = lax.axis_index("dp")
    rep = lax.axis_index("replica")
    rows, width = raw.shape
    length = width // LANES
    block = length // n_rep

    def dp_peer(k):
        return {"dp": lax.rem(dp + k, n_dp)}

    def rep_peer(k):
        return {"replica": lax.rem(rep + k, n_rep)}

    def remote(src, dst, send, recv, peer):
        return pltpu.make_async_remote_copy(
            src_ref=src, dst_ref=dst, send_sem=send, recv_sem=recv,
            device_id=peer, device_id_type=IDS)

    def settle(ref, sem):
        pltpu.make_async_copy(ref, ref, sem.at[0]).wait()

    own = pl.ds(pl.multiple_of(rep * block, block), block)
    offsets = sorted(range(1, n_dp), key=lambda k: abs(2 * k - n_dp))
    grad_load = pltpu.make_async_copy(grad_hbm, raw, load_sem.at[0])
    grad_load.start()

    barrier = pltpu.get_barrier_semaphore()
    for k in offsets:
        pl.semaphore_signal(barrier, inc=1, device_id=dp_peer(k), device_id_type=IDS)
    for k in range(1, n_rep):
        pl.semaphore_signal(barrier, inc=1, device_id=rep_peer(k), device_id_type=IDS)

    state_loads = [
        pltpu.make_async_copy(ref, state.at[i, own], load_sem.at[1 + i])
        for i, ref in enumerate((master_hbm, moment_hbm, second_hbm))
    ]
    for load in state_loads:
        load.start()
    grad_load.wait()
    for t in range(length):
        tile = raw[:, t * LANES:(t + 1) * LANES].astype(jnp.float32)
        tiles[t * rows:(t + 1) * rows, :] = tile
    for k in offsets:
        peer = lax.rem(dp + k, n_dp)
        rows_out[k] = tiles[pl.ds(peer, length, stride=rows), :].astype(jnp.bfloat16)
    for load in state_loads:
        load.wait()
    pl.semaphore_wait(barrier, n_dp + n_rep - 2)

    for k in offsets:
        copy = remote(rows_out.at[k], rows_in.at[k], row_send.at[0], row_recv.at[0], dp_peer(k))
        copy.start()
    for k in range(1, n_rep):
        copy = remote(state.at[:, own], state.at[:, own], state_send.at[0], state_recv.at[0], rep_peer(k))
        copy.start()

    total = tiles[pl.ds(dp, length, stride=rows), :]
    settle(rows_in.at[1:n_dp], row_recv)
    for k in offsets:
        total = total + rows_in[k].astype(jnp.float32)
    parts[rep] = total
    for k in range(1, n_rep):
        copy = remote(parts.at[rep], parts.at[rep], part_send.at[0], part_recv.at[0], rep_peer(k))
        copy.start()

    settle(state.at[:, 0:(n_rep - 1) * block], state_recv)
    master = state[0]
    stats[dp, 1:2] = jnp.sum(master * master, axis=0, keepdims=True)
    old_moment = 0.9 * state[1]
    old_second = 0.999 * state[2]
    settle(rows_out.at[1:n_dp], row_send)
    settle(state.at[:, 0:(n_rep - 1) * block], state_send)
    settle(parts.at[1:n_rep], part_recv)
    summed = parts[0]
    for r in range(1, n_rep):
        summed = summed + parts[r]
    grad = summed * (1.0 / (n_dp * n_rep))
    new_moment = old_moment + 0.1 * grad
    new_second = old_second + 0.001 * grad * grad
    direction = new_moment * FIRST_SCALE / (jnp.sqrt(new_second * SECOND_SCALE) + 1e-08)
    stats[dp, 0:1] = jnp.sum(direction * direction, axis=0, keepdims=True)
    for k in offsets:
        copy = remote(stats.at[dp], stats.at[dp], stat_send.at[0], stat_recv.at[0], dp_peer(k))
        copy.start()

    new_master = master - 0.0003 * (direction + 0.1 * master)
    row_out[...] = new_master
    for i, value in enumerate((new_master, new_moment, new_second, direction)):
        full[i] = value
    for i in range(4):
        blocks_out[i] = full[i, own]
    settle(parts.at[1:n_rep], part_send)

    settle(stats.at[1:n_dp], stat_recv)
    per_mat = rows // MATS
    lane = lax.broadcasted_iota(jnp.int32, (1, LANES), 1)
    ratios = jnp.zeros((1, LANES), jnp.float32)
    for m in range(MATS):
        pair = stats[m * per_mat]
        for r in range(1, per_mat):
            pair = pair + stats[m * per_mat + r]
        norms = jnp.sqrt(jnp.sum(pair, axis=1, keepdims=True))
        ratio = norms[0:1] / (norms[1:2] + 1e-06)
        ratios = jnp.where(lane == m, ratio, ratios)
    ratio_out[...] = ratios

    settle(stats.at[1:n_dp], stat_send)


def by_rows(raw_rows, flat, n_dp, n_rep):
    rows, width = raw_rows.shape
    block = flat[0].shape[0]
    length = width // LANES
    f32 = jnp.float32
    vmem = pl.BlockSpec(memory_space=pltpu.VMEM)
    dma = pltpu.SemaphoreType.DMA
    return pl.pallas_call(
        functools.partial(rows_kernel, n_dp, n_rep),
        out_shape=[
            pltpu.VMEM((length, LANES), f32),
            pltpu.VMEM((4, block, LANES), f32),
            pltpu.VMEM((1, LANES), f32),
        ],
        in_specs=[pl.BlockSpec(memory_space=pl.ANY)] * 4,
        out_specs=[vmem] * 3,
        scratch_shapes=[
            pltpu.VMEM((rows, width), jnp.bfloat16),
            pltpu.VMEM((3, length, LANES), f32),
            pltpu.VMEM((rows * length, LANES), f32),
            pltpu.VMEM((n_dp, length, LANES), jnp.bfloat16),
            pltpu.VMEM((n_dp, length, LANES), jnp.bfloat16),
            pltpu.VMEM((n_rep, length, LANES), f32),
            pltpu.VMEM((4, length, LANES), f32),
            pltpu.VMEM((n_dp, 2, LANES), f32),
            dma((4,)),
            *[dma((1,))] * 8,
        ],
        compiler_params=pltpu.CompilerParams(collective_id=0, has_side_effects=True),
    )(raw_rows, *flat)


def finish(row_ref, blocks_ref, ratio_ref, params_out, master_out, moment_out, second_out, dir_out, ratio_out):
    for t in range(row_ref.shape[0]):
        params_out[:, t * LANES:(t + 1) * LANES] = row_ref[t:t + 1, :].astype(jnp.bfloat16)
    for i, out in enumerate((master_out, moment_out, second_out, dir_out)):
        out[...] = blocks_ref[i]
    ratio_out[...] = ratio_ref[0, :MATS]


def local(gradient, master, moment, second):
    raw_rows = gradient[0, 0]
    rows, width = raw_rows.shape
    n_dp = lax.axis_size("dp")
    n_rep = lax.axis_size("replica")
    cols = master.shape[1]
    block = cols // LANES
    f32 = jnp.float32
    vmem = pl.BlockSpec(memory_space=pltpu.VMEM)
    flat = [a.reshape(block, LANES) for a in (master, moment, second)]
    own_width = width // len(OWNERS)
    gathered = n_dp * n_rep * rows * own_width * 2
    fits = gathered <= DIRECT_BYTES and len(OWNERS) % n_rep == 0 and own_width % (8 * LANES) == 0
    exists = all(d < n_dp and r < n_rep for d, r in OWNERS)
    step = direct if fits and exists and rows == n_dp else by_rows
    row, blocks, ratios = step(raw_rows, flat, n_dp, n_rep)
    row, blocks, ratios = (
        pltpu.with_memory_space_constraint(a, pltpu.VMEM) for a in (row, blocks, ratios))
    outs = pl.pallas_call(
        finish,
        out_shape=[jax.ShapeDtypeStruct((1, width), jnp.bfloat16)]
        + [jax.ShapeDtypeStruct((block, LANES), f32)] * 4
        + [jax.ShapeDtypeStruct((MATS,), f32)],
        in_specs=[vmem] * 3,
        out_specs=[vmem] * 6,
    )(row, blocks, ratios)
    new_params, new_master, new_moment, new_second, direction, ratios = outs
    new_blocks = [a.reshape(1, cols) for a in (new_master, new_moment, new_second, direction)]
    return (new_params, *new_blocks, ratios)


def solution(mesh):
    return jax.shard_map(
        local,
        mesh=mesh,
        in_specs=(
            P("replica", "dp", None, None),
            P("dp", "replica"),
            P("dp", "replica"),
            P("dp", "replica"),
        ),
        out_specs=(
            P("dp", None),
            P("dp", "replica"),
            P("dp", "replica"),
            P("dp", "replica"),
            P("dp", "replica"),
            P(),
        ),
        check_vma=False,
    )
```

```python
import functools

import jax
import jax.numpy as jnp
from jax import lax
from jax.experimental import pallas as pl
from jax.experimental.pallas import tpu as pltpu
from jax.sharding import PartitionSpec as P

MATS = 4
STEP = 2
LANES = 128
IDS = pl.DeviceIdType.MESH
FIRST_SCALE = 1.0 / (1.0 - 0.9**STEP)
SECOND_SCALE = 1.0 / (1.0 - 0.999**STEP)
OWNERS = ((1, 0), (3, 0), (1, 1), (3, 1), (5, 1), (1, 2), (3, 2), (5, 2))
SEND_ORDER = (7, 6, 3, 1, 4, 5, 2, 0)
DIRECT_BYTES = 16 * 2**20


def adam(grad, master, moment, second):
    new_moment = 0.9 * moment + 0.1 * grad
    new_second = 0.999 * second + 0.001 * grad * grad
    direction = new_moment * FIRST_SCALE / (jnp.sqrt(new_second * SECOND_SCALE) + 1e-08)
    new_master = master - 0.0003 * (direction + 0.1 * master)
    return new_master, new_moment, new_second, direction


def direct_kernel(n_dp, n_rep, grad_hbm, master_hbm, moment_hbm, second_hbm,
                  row_out, blocks_out, ratio_out,
                  mine, raw_in, state_in, states, sent, tiles, grad_out, grad_in, msg_out, msg_in,
                  load_sem, raw_send, raw_recv, state_send, state_recv,
                  grad_send, grad_recv, msg_send, msg_recv):
    dp = lax.axis_index("dp")
    rep = lax.axis_index("replica")
    n_own = len(OWNERS)
    per = n_own // n_rep
    rows, width = grad_hbm.shape
    wide = width // n_own
    block = wide // LANES
    f32 = jnp.float32

    def settle(ref, sem):
        pltpu.make_async_copy(ref, ref, sem).wait()

    def remote(src, dst, send, recv, device):
        return pltpu.make_async_remote_copy(
            src_ref=src, dst_ref=dst, send_sem=send, recv_sem=recv,
            device_id=device, device_id_type=IDS)

    def copy_to(here, src, dst, send, recv, device):
        @pl.when(here)
        def _():
            pltpu.make_async_copy(src, dst, recv).start()

        @pl.when(jnp.logical_not(here))
        def _():
            remote(src, dst, send, recv, device).start()

    is_me = [(dp == d) & (rep == r) for d, r in OWNERS]
    owner = functools.reduce(jnp.logical_or, is_me)
    index = sum(b * m.astype(jnp.int32) for b, m in enumerate(is_me))

    barrier = pltpu.get_barrier_semaphore()

    @pl.when(owner)
    def _():
        for r in sorted(range(n_rep), key=lambda r: -min(r, n_rep - r)):
            for k in range(n_dp):
                if k or r:
                    pl.semaphore_signal(
                        barrier, inc=1, device_id=(lax.rem(dp + k, n_dp), lax.rem(rep + r, n_rep)),
                        device_id_type=IDS)

    state_hbm = (master_hbm, moment_hbm, second_hbm)
    loads = [pltpu.make_async_copy(ref, mine.at[i], load_sem.at[0]) for i, ref in enumerate(state_hbm)]
    for load in loads:
        load.start()
    with jax.named_scope("enter"):
        pl.semaphore_wait(barrier, n_own - owner.astype(jnp.int32))

    for b, device in enumerate(OWNERS):
        @pl.when(rep == b // per)
        def _():
            sub = b % per
            for i, ref in enumerate(state_hbm):
                copy_to(is_me[b], ref.at[sub * block:(sub + 1) * block], state_in.at[i, dp],
                        state_send.at[0], state_recv.at[0], device)

    slot = rep * n_dp + dp
    for b in SEND_ORDER:
        device = OWNERS[b]
        copy_to(is_me[b], grad_hbm.at[:, b * wide:(b + 1) * wide], raw_in.at[slot],
                raw_send.at[0], raw_recv.at[rep], device)
    lane = lax.broadcasted_iota(jnp.int32, (block, LANES), 1)

    def squares(v):
        per_mat = rows // MATS
        spread = jnp.zeros((block, LANES), f32)
        for m in range(MATS):
            part = sum(v[r] * v[r] for r in range(m * per_mat, (m + 1) * per_mat))
            spread = jnp.where(lane == m, jnp.sum(part, axis=1, keepdims=True), spread)
        return jnp.sum(spread, axis=0, keepdims=True)

    @pl.when(owner)
    def _():
        total = None
        planes = (1, 0, *range(2, n_rep))
        for z in planes:
            if z == planes[-1]:
                with jax.named_scope("wait_state"):
                    settle(state_in, state_recv.at[0])
                master, moment, second = (state_in[i] for i in range(3))
                weights = squares(master)
                for r in range(rows):
                    msg_out[r, block + 1:block + 2] = weights
            with jax.named_scope(f"wait_raw{z}"):
                settle(raw_in.at[z * n_dp:(z + 1) * n_dp], raw_recv.at[z])
            for s in range(z * n_dp, (z + 1) * n_dp):
                part = raw_in[s].astype(f32)
                total = part if total is None else total + part
        total = total * (1.0 / (n_dp * n_rep))
        for t in range(block):
            tiles[t * rows:(t + 1) * rows, :] = total[:, t * LANES:(t + 1) * LANES]
        for r in range(rows):
            grad_out[r] = tiles[pl.ds(r, block, stride=rows), :]
        new_master, _, _, direction = adam(grad_out[...], master, moment, second)
        moved = squares(direction)
        for r in range(rows):
            msg_out[r, 0:block] = new_master[r]
            msg_out[r, block:block + 1] = moved
        place = index // per
        targets = [(r, z) for z in (0, *reversed(range(1, n_rep))) for r in range(rows)]
        for n, (r, z) in enumerate(targets):
            if n == 2:
                for s in range(rows):
                    copy_to((dp == s) & (rep == place), grad_out.at[s], grad_in.at[lax.rem(index, per)],
                            grad_send.at[0], grad_recv.at[0], (s, place))
            copy_to((dp == r) & (rep == z), msg_out.at[r], msg_in.at[index],
                    msg_send.at[0], msg_recv.at[0], (r, z))

    settle(mine, load_sem.at[0])
    keeps = functools.reduce(jnp.logical_or, [m & (rep == b // per) for b, m in enumerate(is_me)])

    def settle_sent(ref, sem, one_less):
        count = ref.shape[0]

        @pl.when(one_less)
        def _():
            settle(ref.at[0:count - 1], sem)

        @pl.when(jnp.logical_not(one_less))
        def _():
            settle(ref, sem)

    settle_sent(raw_in.at[0:n_own], raw_send.at[0], owner)
    settle_sent(states.at[0:per], state_send.at[0], keeps)
    with jax.named_scope("wait_grad"):
        settle(grad_in, grad_recv.at[0])
    grad = grad_in[...].reshape(per * block, LANES)
    for i, value in enumerate(adam(grad, mine[0], mine[1], mine[2])):
        blocks_out[i] = value
    with jax.named_scope("wait_msg"):
        settle(msg_in, msg_recv.at[0])
    norms = jnp.zeros((2, LANES), f32)
    for b in range(n_own):
        row_out[b * block:(b + 1) * block] = msg_in[b, 0:block]
        norms = norms + msg_in[b, block:]
    norms = jnp.sqrt(norms)
    ratio_out[...] = norms[0:1] / (norms[1:2] + 1e-06)

    @pl.when(owner)
    def _():
        settle_sent(grad_out, grad_send.at[0], rep == index // per)
        settle(sent, msg_send.at[0])


def direct(raw_rows, flat, n_dp, n_rep):
    rows, width = raw_rows.shape
    n_own = len(OWNERS)
    per = n_own // n_rep
    length, wide = width // LANES, width // n_own
    block = wide // LANES
    f32 = jnp.float32
    dma = pltpu.SemaphoreType.DMA
    return pl.pallas_call(
        functools.partial(direct_kernel, n_dp, n_rep),
        out_shape=[
            pltpu.VMEM((length, LANES), f32),
            pltpu.VMEM((4, per * block, LANES), f32),
            pltpu.VMEM((1, LANES), f32),
        ],
        in_specs=[pl.BlockSpec(memory_space=pl.ANY)] * 4,
        out_specs=[pl.BlockSpec(memory_space=pltpu.VMEM)] * 3,
        scratch_shapes=[
            pltpu.VMEM((3, per * block, LANES), f32),
            pltpu.VMEM((n_dp * n_rep, rows, wide), jnp.bfloat16),
            pltpu.VMEM((3, rows, block, LANES), f32),
            pltpu.VMEM((per, 3, block, LANES), f32),
            pltpu.VMEM((n_dp * n_rep - 1, block + 2, LANES), f32),
            pltpu.VMEM((rows * block, LANES), f32),
            pltpu.VMEM((rows, block, LANES), f32),
            pltpu.VMEM((per, block, LANES), f32),
            pltpu.VMEM((rows, block + 2, LANES), f32),
            pltpu.VMEM((n_own, block + 2, LANES), f32),
            dma((1,)), dma((1,)), dma((n_rep,)), *[dma((1,))] * 6,
        ],
        compiler_params=pltpu.CompilerParams(collective_id=0, has_side_effects=True),
    )(raw_rows, *flat)


def rows_kernel(n_dp, n_rep, grad_hbm, master_hbm, moment_hbm, second_hbm,
                row_out, blocks_out, ratio_out,
                raw, state, tiles, rows_out, rows_in, parts, full, stats,
                load_sem, state_send, state_recv, row_send, row_recv,
                part_send, part_recv, stat_send, stat_recv):
    dp = lax.axis_index("dp")
    rep = lax.axis_index("replica")
    rows, width = raw.shape
    length = width // LANES
    block = length // n_rep

    def dp_peer(k):
        return {"dp": lax.rem(dp + k, n_dp)}

    def rep_peer(k):
        return {"replica": lax.rem(rep + k, n_rep)}

    def remote(src, dst, send, recv, peer):
        return pltpu.make_async_remote_copy(
            src_ref=src, dst_ref=dst, send_sem=send, recv_sem=recv,
            device_id=peer, device_id_type=IDS)

    def settle(ref, sem):
        pltpu.make_async_copy(ref, ref, sem.at[0]).wait()

    own = pl.ds(pl.multiple_of(rep * block, block), block)
    offsets = sorted(range(1, n_dp), key=lambda k: abs(2 * k - n_dp))
    grad_load = pltpu.make_async_copy(grad_hbm, raw, load_sem.at[0])
    grad_load.start()

    barrier = pltpu.get_barrier_semaphore()
    for k in offsets:
        pl.semaphore_signal(barrier, inc=1, device_id=dp_peer(k), device_id_type=IDS)
    for k in range(1, n_rep):
        pl.semaphore_signal(barrier, inc=1, device_id=rep_peer(k), device_id_type=IDS)

    state_loads = [
        pltpu.make_async_copy(ref, state.at[i, own], load_sem.at[1 + i])
        for i, ref in enumerate((master_hbm, moment_hbm, second_hbm))
    ]
    for load in state_loads:
        load.start()
    grad_load.wait()
    for t in range(length):
        tile = raw[:, t * LANES:(t + 1) * LANES].astype(jnp.float32)
        tiles[t * rows:(t + 1) * rows, :] = tile
    for k in offsets:
        peer = lax.rem(dp + k, n_dp)
        rows_out[k] = tiles[pl.ds(peer, length, stride=rows), :].astype(jnp.bfloat16)
    for load in state_loads:
        load.wait()
    pl.semaphore_wait(barrier, n_dp + n_rep - 2)

    for k in offsets:
        copy = remote(rows_out.at[k], rows_in.at[k], row_send.at[0], row_recv.at[0], dp_peer(k))
        copy.start()
    for k in range(1, n_rep):
        copy = remote(state.at[:, own], state.at[:, own], state_send.at[0], state_recv.at[0], rep_peer(k))
        copy.start()

    total = tiles[pl.ds(dp, length, stride=rows), :]
    settle(rows_in.at[1:n_dp], row_recv)
    for k in offsets:
        total = total + rows_in[k].astype(jnp.float32)
    parts[rep] = total
    for k in range(1, n_rep):
        copy = remote(parts.at[rep], parts.at[rep], part_send.at[0], part_recv.at[0], rep_peer(k))
        copy.start()

    settle(state.at[:, 0:(n_rep - 1) * block], state_recv)
    master = state[0]
    stats[dp, 1:2] = jnp.sum(master * master, axis=0, keepdims=True)
    old_moment = 0.9 * state[1]
    old_second = 0.999 * state[2]
    settle(rows_out.at[1:n_dp], row_send)
    settle(state.at[:, 0:(n_rep - 1) * block], state_send)
    settle(parts.at[1:n_rep], part_recv)
    summed = parts[0]
    for r in range(1, n_rep):
        summed = summed + parts[r]
    grad = summed * (1.0 / (n_dp * n_rep))
    new_moment = old_moment + 0.1 * grad
    new_second = old_second + 0.001 * grad * grad
    direction = new_moment * FIRST_SCALE / (jnp.sqrt(new_second * SECOND_SCALE) + 1e-08)
    stats[dp, 0:1] = jnp.sum(direction * direction, axis=0, keepdims=True)
    for k in offsets:
        copy = remote(stats.at[dp], stats.at[dp], stat_send.at[0], stat_recv.at[0], dp_peer(k))
        copy.start()

    new_master = master - 0.0003 * (direction + 0.1 * master)
    row_out[...] = new_master
    for i, value in enumerate((new_master, new_moment, new_second, direction)):
        full[i] = value
    for i in range(4):
        blocks_out[i] = full[i, own]
    settle(parts.at[1:n_rep], part_send)

    settle(stats.at[1:n_dp], stat_recv)
    per_mat = rows // MATS
    lane = lax.broadcasted_iota(jnp.int32, (1, LANES), 1)
    ratios = jnp.zeros((1, LANES), jnp.float32)
    for m in range(MATS):
        pair = stats[m * per_mat]
        for r in range(1, per_mat):
            pair = pair + stats[m * per_mat + r]
        norms = jnp.sqrt(jnp.sum(pair, axis=1, keepdims=True))
        ratio = norms[0:1] / (norms[1:2] + 1e-06)
        ratios = jnp.where(lane == m, ratio, ratios)
    ratio_out[...] = ratios

    settle(stats.at[1:n_dp], stat_send)


def by_rows(raw_rows, flat, n_dp, n_rep):
    rows, width = raw_rows.shape
    block = flat[0].shape[0]
    length = width // LANES
    f32 = jnp.float32
    vmem = pl.BlockSpec(memory_space=pltpu.VMEM)
    dma = pltpu.SemaphoreType.DMA
    return pl.pallas_call(
        functools.partial(rows_kernel, n_dp, n_rep),
        out_shape=[
            pltpu.VMEM((length, LANES), f32),
            pltpu.VMEM((4, block, LANES), f32),
            pltpu.VMEM((1, LANES), f32),
        ],
        in_specs=[pl.BlockSpec(memory_space=pl.ANY)] * 4,
        out_specs=[vmem] * 3,
        scratch_shapes=[
            pltpu.VMEM((rows, width), jnp.bfloat16),
            pltpu.VMEM((3, length, LANES), f32),
            pltpu.VMEM((rows * length, LANES), f32),
            pltpu.VMEM((n_dp, length, LANES), jnp.bfloat16),
            pltpu.VMEM((n_dp, length, LANES), jnp.bfloat16),
            pltpu.VMEM((n_rep, length, LANES), f32),
            pltpu.VMEM((4, length, LANES), f32),
            pltpu.VMEM((n_dp, 2, LANES), f32),
            dma((4,)),
            *[dma((1,))] * 8,
        ],
        compiler_params=pltpu.CompilerParams(collective_id=0, has_side_effects=True),
    )(raw_rows, *flat)


def finish(row_ref, blocks_ref, ratio_ref, params_out, master_out, moment_out, second_out, dir_out, ratio_out):
    for t in range(row_ref.shape[0]):
        params_out[:, t * LANES:(t + 1) * LANES] = row_ref[t:t + 1, :].astype(jnp.bfloat16)
    for i, out in enumerate((master_out, moment_out, second_out, dir_out)):
        out[...] = blocks_ref[i]
    ratio_out[...] = ratio_ref[0, :MATS]


def local(gradient, master, moment, second):
    raw_rows = gradient[0, 0]
    rows, width = raw_rows.shape
    n_dp = lax.axis_size("dp")
    n_rep = lax.axis_size("replica")
    cols = master.shape[1]
    block = cols // LANES
    f32 = jnp.float32
    vmem = pl.BlockSpec(memory_space=pltpu.VMEM)
    flat = [a.reshape(block, LANES) for a in (master, moment, second)]
    own_width = width // len(OWNERS)
    gathered = n_dp * n_rep * rows * own_width * 2
    fits = gathered <= DIRECT_BYTES and len(OWNERS) % n_rep == 0 and own_width % (8 * LANES) == 0
    exists = all(d < n_dp and r < n_rep for d, r in OWNERS)
    step = direct if fits and exists and rows == n_dp else by_rows
    row, blocks, ratios = step(raw_rows, flat, n_dp, n_rep)
    row, blocks, ratios = (
        pltpu.with_memory_space_constraint(a, pltpu.VMEM) for a in (row, blocks, ratios))
    outs = pl.pallas_call(
        finish,
        out_shape=[jax.ShapeDtypeStruct((1, width), jnp.bfloat16)]
        + [jax.ShapeDtypeStruct((block, LANES), f32)] * 4
        + [jax.ShapeDtypeStruct((MATS,), f32)],
        in_specs=[vmem] * 3,
        out_specs=[vmem] * 6,
    )(row, blocks, ratios)
    new_params, new_master, new_moment, new_second, direction, ratios = outs
    new_blocks = [a.reshape(1, cols) for a in (new_master, new_moment, new_second, direction)]
    return (new_params, *new_blocks, ratios)


def solution(mesh):
    return jax.shard_map(
        local,
        mesh=mesh,
        in_specs=(
            P("replica", "dp", None, None),
            P("dp", "replica"),
            P("dp", "replica"),
            P("dp", "replica"),
        ),
        out_specs=(
            P("dp", None),
            P("dp", "replica"),
            P("dp", "replica"),
            P("dp", "replica"),
            P("dp", "replica"),
            P(),
        ),
        check_vma=False,
    )
```

```python
import functools

import jax
import jax.numpy as jnp
from jax import lax
from jax.experimental import pallas as pl
from jax.experimental.pallas import tpu as pltpu
from jax.sharding import PartitionSpec as P

MATS = 4
STEP = 2
LANES = 128
IDS = pl.DeviceIdType.MESH
FIRST_SCALE = 1.0 / (1.0 - 0.9**STEP)
SECOND_SCALE = 1.0 / (1.0 - 0.999**STEP)
OWNERS = ((1, 0), (3, 0), (1, 1), (3, 1), (5, 1), (1, 2), (3, 2), (5, 2))
DIRECT_BYTES = 16 * 2**20


def hops(a, b):
    (u, p), (v, q) = a, b
    return abs(u // 2 % 2 - v // 2 % 2) + abs(u // 4 - v // 4) + abs(p - q)


def send_order(place):
    back = [hops(device, (0, 0)) for device in OWNERS]
    ties = (7, 6, 3, 1, 4, 5, 2, 0)
    return tuple(sorted(range(len(OWNERS)), key=lambda b: (-hops(place, OWNERS[b]) - 0.2 * back[b], ties.index(b))))


def adam(grad, master, moment, second):
    new_moment = 0.9 * moment + 0.1 * grad
    new_second = 0.999 * second + 0.001 * grad * grad
    direction = new_moment * FIRST_SCALE / (jnp.sqrt(new_second * SECOND_SCALE) + 1e-08)
    new_master = master - 0.0003 * (direction + 0.1 * master)
    return new_master, new_moment, new_second, direction


def direct_kernel(n_dp, n_rep, grad_hbm, master_hbm, moment_hbm, second_hbm,
                  row_out, blocks_out, ratio_out,
                  mine, raw_in, state_in, rows_of, grad_out, grad_in, msg_out, msg_in,
                  load_sem, send_sem, raw_recv, state_recv, result_recv):
    dp = lax.axis_index("dp")
    rep = lax.axis_index("replica")
    n_own = len(OWNERS)
    per = n_own // n_rep
    rows, width = grad_hbm.shape
    wide = width // n_own
    block = wide // LANES
    f32 = jnp.float32

    def settle(ref, sem):
        pltpu.make_async_copy(ref, ref, sem).wait()

    def settle_rows(count, sem):
        settle(rows_of.at[0:count], sem)

    def remote(src, dst, send, recv, device):
        return pltpu.make_async_remote_copy(
            src_ref=src, dst_ref=dst, send_sem=send, recv_sem=recv,
            device_id=device, device_id_type=IDS)

    def copy_to(here, src, dst, send, recv, device):
        @pl.when(here)
        def _():
            pltpu.make_async_copy(src, dst, recv).start()

        @pl.when(jnp.logical_not(here))
        def _():
            remote(src, dst, send, recv, device).start()

    is_me = [(dp == d) & (rep == r) for d, r in OWNERS]
    owner = functools.reduce(jnp.logical_or, is_me)
    index = sum(b * m.astype(jnp.int32) for b, m in enumerate(is_me))

    barrier = pltpu.get_barrier_semaphore()

    @pl.when(owner)
    def _():
        for r in sorted(range(n_rep), key=lambda r: -min(r, n_rep - r)):
            for k in range(n_dp):
                if k or r:
                    pl.semaphore_signal(
                        barrier, inc=1, device_id=(lax.rem(dp + k, n_dp), lax.rem(rep + r, n_rep)),
                        device_id_type=IDS)

    state_hbm = (master_hbm, moment_hbm, second_hbm)
    loads = [pltpu.make_async_copy(ref, mine.at[i], load_sem.at[0]) for i, ref in enumerate(state_hbm)]
    for load in loads:
        load.start()
    with jax.named_scope("enter"):
        pl.semaphore_wait(barrier, n_own - owner.astype(jnp.int32))

    place = pl.ds(pl.multiple_of(dp * block, block), block)
    for b, device in enumerate(OWNERS):
        @pl.when(rep == b // per)
        def _():
            sub = b % per
            for i, ref in enumerate(state_hbm):
                copy_to(is_me[b], ref.at[sub * block:(sub + 1) * block], state_in.at[i, place],
                        send_sem.at[0], state_recv.at[0], device)

    slot = rep * n_dp + dp
    orders = {}
    for d in range(0, n_dp, 2):
        for r in range(n_rep):
            orders.setdefault(send_order((d, r)), []).append((dp // 2 == d // 2) & (rep == r))
    for order, places in orders.items():
        @pl.when(functools.reduce(jnp.logical_or, places))
        def _():
            for b in order:
                copy_to(is_me[b], grad_hbm.at[:, b * wide:(b + 1) * wide], raw_in.at[slot],
                        send_sem.at[0], raw_recv.at[rep // (n_rep - 1)], OWNERS[b])

    lane = lax.broadcasted_iota(jnp.int32, (rows, LANES), 1)
    mat = lax.broadcasted_iota(jnp.int32, (rows, LANES), 0) // (rows // MATS)

    def squares(parts):
        total = sum(v * v for v in parts)
        spread = jnp.where(lane == mat, jnp.sum(total, axis=1, keepdims=True), 0.0)
        return jnp.broadcast_to(jnp.sum(spread, axis=0, keepdims=True), (rows, LANES))

    @pl.when(owner)
    def _():
        early = (n_rep - 1) * n_dp
        with jax.named_scope("wait_state"):
            settle(state_in, state_recv.at[0])
        state = [[state_in[i, pl.ds(t, rows, stride=block), :] for i in range(3)] for t in range(block)]
        msg_out[block + 1] = squares([master for master, _, _ in state])
        with jax.named_scope("wait_early"):
            settle(raw_in.at[0:early], raw_recv.at[0])
        total = raw_in[0].astype(f32)
        for s in range(1, early):
            total = total + raw_in[s].astype(f32)
        with jax.named_scope("wait_late"):
            settle(raw_in.at[early:], raw_recv.at[1])
        for s in range(early, n_dp * n_rep):
            total = total + raw_in[s].astype(f32)
        total = total * (1.0 / (n_dp * n_rep))
        moved = []
        for t, (master, moment, second) in enumerate(state):
            grad = total[:, t * LANES:(t + 1) * LANES]
            grad_out[t] = grad
            msg_out[t], _, _, direction = adam(grad, master, moment, second)
            moved.append(direction)
        msg_out[block] = squares(moved)
        home = index // per
        targets = [(r, z) for z in range(n_rep) for r in range(rows)]
        for n, (r, z) in enumerate(targets):
            if n == 2:
                for s in range(rows):
                    copy_to((dp == s) & (rep == home), grad_out.at[:, s], grad_in.at[lax.rem(index, per)],
                            send_sem.at[0], result_recv.at[0], (s, home))
            copy_to((dp == r) & (rep == z), msg_out.at[:, r], msg_in.at[index],
                    send_sem.at[0], result_recv.at[0], (r, z))

    settle(mine, load_sem.at[0])
    with jax.named_scope("wait_results"):
        settle_rows(per * block + n_own * (block + 2), result_recv.at[0])
    for i, value in enumerate(adam(grad_in[...].reshape(per * block, LANES), mine[0], mine[1], mine[2])):
        blocks_out[i] = value
    norms = jnp.zeros((2, LANES), f32)
    for b in range(n_own):
        row_out[b * block:(b + 1) * block] = msg_in[b, 0:block]
        norms = norms + msg_in[b, block:]
    norms = jnp.sqrt(norms)
    ratio_out[...] = norms[0:1] / (norms[1:2] + 1e-06)

    raw_rows = rows * wide * 2 // (LANES * 4)
    state_rows = 3 * block
    owned = (n_own - 1) * raw_rows + rows * block + (n_dp * n_rep - 1) * (block + 2)
    at_home = rep == index // per

    @pl.when(jnp.logical_not(owner))
    def _():
        settle_rows(n_own * raw_rows + per * state_rows, send_sem.at[0])

    @pl.when(owner & at_home)
    def _():
        settle_rows(owned + (per - 1) * state_rows - block, send_sem.at[0])

    @pl.when(owner & jnp.logical_not(at_home))
    def _():
        settle_rows(owned + per * state_rows, send_sem.at[0])


def direct(raw_rows, flat, n_dp, n_rep):
    rows, width = raw_rows.shape
    n_own = len(OWNERS)
    per = n_own // n_rep
    length, wide = width // LANES, width // n_own
    block = wide // LANES
    f32 = jnp.float32
    dma = pltpu.SemaphoreType.DMA
    count = n_own * rows * wide // 256 + (3 * per + rows) * block + n_dp * n_rep * (block + 2)
    return pl.pallas_call(
        functools.partial(direct_kernel, n_dp, n_rep),
        out_shape=[
            pltpu.VMEM((length, LANES), f32),
            pltpu.VMEM((4, per * block, LANES), f32),
            pltpu.VMEM((1, LANES), f32),
        ],
        in_specs=[pl.BlockSpec(memory_space=pl.ANY)] * 4,
        out_specs=[pl.BlockSpec(memory_space=pltpu.VMEM)] * 3,
        scratch_shapes=[
            pltpu.VMEM((3, per * block, LANES), f32),
            pltpu.VMEM((n_dp * n_rep, rows, wide), jnp.bfloat16),
            pltpu.VMEM((3, rows * block, LANES), f32),
            pltpu.VMEM((count, LANES), f32),
            pltpu.VMEM((block, rows, LANES), f32),
            pltpu.VMEM((per, block, LANES), f32),
            pltpu.VMEM((block + 2, rows, LANES), f32),
            pltpu.VMEM((n_own, block + 2, LANES), f32),
            dma((1,)), dma((1,)), dma((2,)), dma((1,)), dma((1,)),
        ],
        compiler_params=pltpu.CompilerParams(collective_id=0, has_side_effects=True),
    )(raw_rows, *flat)


def rows_kernel(n_dp, n_rep, grad_hbm, master_hbm, moment_hbm, second_hbm,
                row_out, blocks_out, ratio_out,
                raw, state, tiles, rows_out, rows_in, parts, full, stats,
                load_sem, state_send, state_recv, row_send, row_recv,
                part_send, part_recv, stat_send, stat_recv):
    dp = lax.axis_index("dp")
    rep = lax.axis_index("replica")
    rows, width = raw.shape
    length = width // LANES
    block = length // n_rep

    def dp_peer(k):
        return {"dp": lax.rem(dp + k, n_dp)}

    def rep_peer(k):
        return {"replica": lax.rem(rep + k, n_rep)}

    def remote(src, dst, send, recv, peer):
        return pltpu.make_async_remote_copy(
            src_ref=src, dst_ref=dst, send_sem=send, recv_sem=recv,
            device_id=peer, device_id_type=IDS)

    def settle(ref, sem):
        pltpu.make_async_copy(ref, ref, sem.at[0]).wait()

    own = pl.ds(pl.multiple_of(rep * block, block), block)
    offsets = sorted(range(1, n_dp), key=lambda k: abs(2 * k - n_dp))
    grad_load = pltpu.make_async_copy(grad_hbm, raw, load_sem.at[0])
    grad_load.start()

    barrier = pltpu.get_barrier_semaphore()
    for k in offsets:
        pl.semaphore_signal(barrier, inc=1, device_id=dp_peer(k), device_id_type=IDS)
    for k in range(1, n_rep):
        pl.semaphore_signal(barrier, inc=1, device_id=rep_peer(k), device_id_type=IDS)

    state_loads = [
        pltpu.make_async_copy(ref, state.at[i, own], load_sem.at[1 + i])
        for i, ref in enumerate((master_hbm, moment_hbm, second_hbm))
    ]
    for load in state_loads:
        load.start()
    grad_load.wait()
    for t in range(length):
        tile = raw[:, t * LANES:(t + 1) * LANES].astype(jnp.float32)
        tiles[t * rows:(t + 1) * rows, :] = tile
    for k in offsets:
        peer = lax.rem(dp + k, n_dp)
        rows_out[k] = tiles[pl.ds(peer, length, stride=rows), :].astype(jnp.bfloat16)
    for load in state_loads:
        load.wait()
    pl.semaphore_wait(barrier, n_dp + n_rep - 2)

    for k in offsets:
        copy = remote(rows_out.at[k], rows_in.at[k], row_send.at[0], row_recv.at[0], dp_peer(k))
        copy.start()
    for k in range(1, n_rep):
        copy = remote(state.at[:, own], state.at[:, own], state_send.at[0], state_recv.at[0], rep_peer(k))
        copy.start()

    total = tiles[pl.ds(dp, length, stride=rows), :]
    settle(rows_in.at[1:n_dp], row_recv)
    for k in offsets:
        total = total + rows_in[k].astype(jnp.float32)
    parts[rep] = total
    for k in range(1, n_rep):
        copy = remote(parts.at[rep], parts.at[rep], part_send.at[0], part_recv.at[0], rep_peer(k))
        copy.start()

    settle(state.at[:, 0:(n_rep - 1) * block], state_recv)
    master = state[0]
    stats[dp, 1:2] = jnp.sum(master * master, axis=0, keepdims=True)
    old_moment = 0.9 * state[1]
    old_second = 0.999 * state[2]
    settle(rows_out.at[1:n_dp], row_send)
    settle(state.at[:, 0:(n_rep - 1) * block], state_send)
    settle(parts.at[1:n_rep], part_recv)
    summed = parts[0]
    for r in range(1, n_rep):
        summed = summed + parts[r]
    grad = summed * (1.0 / (n_dp * n_rep))
    new_moment = old_moment + 0.1 * grad
    new_second = old_second + 0.001 * grad * grad
    direction = new_moment * FIRST_SCALE / (jnp.sqrt(new_second * SECOND_SCALE) + 1e-08)
    stats[dp, 0:1] = jnp.sum(direction * direction, axis=0, keepdims=True)
    for k in offsets:
        copy = remote(stats.at[dp], stats.at[dp], stat_send.at[0], stat_recv.at[0], dp_peer(k))
        copy.start()

    new_master = master - 0.0003 * (direction + 0.1 * master)
    row_out[...] = new_master
    for i, value in enumerate((new_master, new_moment, new_second, direction)):
        full[i] = value
    for i in range(4):
        blocks_out[i] = full[i, own]
    settle(parts.at[1:n_rep], part_send)

    settle(stats.at[1:n_dp], stat_recv)
    per_mat = rows // MATS
    lane = lax.broadcasted_iota(jnp.int32, (1, LANES), 1)
    ratios = jnp.zeros((1, LANES), jnp.float32)
    for m in range(MATS):
        pair = stats[m * per_mat]
        for r in range(1, per_mat):
            pair = pair + stats[m * per_mat + r]
        norms = jnp.sqrt(jnp.sum(pair, axis=1, keepdims=True))
        ratio = norms[0:1] / (norms[1:2] + 1e-06)
        ratios = jnp.where(lane == m, ratio, ratios)
    ratio_out[...] = ratios

    settle(stats.at[1:n_dp], stat_send)


def by_rows(raw_rows, flat, n_dp, n_rep):
    rows, width = raw_rows.shape
    block = flat[0].shape[0]
    length = width // LANES
    f32 = jnp.float32
    vmem = pl.BlockSpec(memory_space=pltpu.VMEM)
    dma = pltpu.SemaphoreType.DMA
    return pl.pallas_call(
        functools.partial(rows_kernel, n_dp, n_rep),
        out_shape=[
            pltpu.VMEM((length, LANES), f32),
            pltpu.VMEM((4, block, LANES), f32),
            pltpu.VMEM((1, LANES), f32),
        ],
        in_specs=[pl.BlockSpec(memory_space=pl.ANY)] * 4,
        out_specs=[vmem] * 3,
        scratch_shapes=[
            pltpu.VMEM((rows, width), jnp.bfloat16),
            pltpu.VMEM((3, length, LANES), f32),
            pltpu.VMEM((rows * length, LANES), f32),
            pltpu.VMEM((n_dp, length, LANES), jnp.bfloat16),
            pltpu.VMEM((n_dp, length, LANES), jnp.bfloat16),
            pltpu.VMEM((n_rep, length, LANES), f32),
            pltpu.VMEM((4, length, LANES), f32),
            pltpu.VMEM((n_dp, 2, LANES), f32),
            dma((4,)),
            *[dma((1,))] * 8,
        ],
        compiler_params=pltpu.CompilerParams(collective_id=0, has_side_effects=True),
    )(raw_rows, *flat)


def finish(row_ref, blocks_ref, ratio_ref, params_out, master_out, moment_out, second_out, dir_out, ratio_out):
    for t in range(row_ref.shape[0]):
        params_out[:, t * LANES:(t + 1) * LANES] = row_ref[t:t + 1, :].astype(jnp.bfloat16)
    for i, out in enumerate((master_out, moment_out, second_out, dir_out)):
        out[...] = blocks_ref[i]
    ratio_out[...] = ratio_ref[0, :MATS]


def local(gradient, master, moment, second):
    raw_rows = gradient[0, 0]
    rows, width = raw_rows.shape
    n_dp = lax.axis_size("dp")
    n_rep = lax.axis_size("replica")
    cols = master.shape[1]
    block = cols // LANES
    f32 = jnp.float32
    vmem = pl.BlockSpec(memory_space=pltpu.VMEM)
    flat = [a.reshape(block, LANES) for a in (master, moment, second)]
    own_width = width // len(OWNERS)
    gathered = n_dp * n_rep * rows * own_width * 2
    fits = gathered <= DIRECT_BYTES and len(OWNERS) % n_rep == 0 and own_width % (8 * LANES) == 0
    exists = all(d < n_dp and r < n_rep for d, r in OWNERS)
    step = direct if fits and exists and rows == n_dp else by_rows
    row, blocks, ratios = step(raw_rows, flat, n_dp, n_rep)
    row, blocks, ratios = (
        pltpu.with_memory_space_constraint(a, pltpu.VMEM) for a in (row, blocks, ratios))
    outs = pl.pallas_call(
        finish,
        out_shape=[jax.ShapeDtypeStruct((1, width), jnp.bfloat16)]
        + [jax.ShapeDtypeStruct((block, LANES), f32)] * 4
        + [jax.ShapeDtypeStruct((MATS,), f32)],
        in_specs=[vmem] * 3,
        out_specs=[vmem] * 6,
    )(row, blocks, ratios)
    new_params, new_master, new_moment, new_second, direction, ratios = outs
    new_blocks = [a.reshape(1, cols) for a in (new_master, new_moment, new_second, direction)]
    return (new_params, *new_blocks, ratios)


def solution(mesh):
    return jax.shard_map(
        local,
        mesh=mesh,
        in_specs=(
            P("replica", "dp", None, None),
            P("dp", "replica"),
            P("dp", "replica"),
            P("dp", "replica"),
        ),
        out_specs=(
            P("dp", None),
            P("dp", "replica"),
            P("dp", "replica"),
            P("dp", "replica"),
            P("dp", "replica"),
            P(),
        ),
        check_vma=False,
    )
```

```python
import functools

import jax
import jax.numpy as jnp
from jax import lax
from jax.experimental import pallas as pl
from jax.experimental.pallas import tpu as pltpu
from jax.sharding import PartitionSpec as P

MATS = 4
STEP = 2
LANES = 128
IDS = pl.DeviceIdType.MESH
FIRST_SCALE = 1.0 / (1.0 - 0.9**STEP)
SECOND_SCALE = 1.0 / (1.0 - 0.999**STEP)
OWNERS = ((1, 0), (3, 0), (1, 1), (3, 1), (1, 2), (5, 1), (3, 2), (5, 2))
LEAD = (1.1, 0.2, 0.2, 1.5, 0.4, 1.0, 0.6, 0.6)
DIRECT_BYTES = 16 * 2**20


def hops(a, b):
    (u, p), (v, q) = a, b
    return abs(u // 2 % 2 - v // 2 % 2) + abs(u // 4 - v // 4) + abs(p - q)


def send_order(place):
    ties = (7, 6, 3, 1, 5, 4, 2, 0)
    return tuple(sorted(range(len(OWNERS)), key=lambda b: (-hops(place, OWNERS[b]) - LEAD[b], ties.index(b))))


def adam(grad, master, moment, second):
    new_moment = 0.9 * moment + 0.1 * grad
    new_second = 0.999 * second + 0.001 * grad * grad
    direction = new_moment * FIRST_SCALE / (jnp.sqrt(new_second * SECOND_SCALE) + 1e-08)
    new_master = master - 0.0003 * (direction + 0.1 * master)
    return new_master, new_moment, new_second, direction


def direct_kernel(n_dp, n_rep, grad_hbm, master_hbm, moment_hbm, second_hbm,
                  row_out, blocks_out, ratio_out,
                  mine, raw_in, state_in, rows_of, grad_out, grad_in, msg_out, msg_in,
                  load_sem, send_sem, raw_recv, state_recv, result_recv):
    dp = lax.axis_index("dp")
    rep = lax.axis_index("replica")
    n_own = len(OWNERS)
    per = n_own // n_rep
    rows, width = grad_hbm.shape
    wide = width // n_own
    block = wide // LANES
    f32 = jnp.float32

    def settle(ref, sem):
        pltpu.make_async_copy(ref, ref, sem).wait()

    def settle_rows(count, sem):
        settle(rows_of.at[0:count], sem)

    def remote(src, dst, send, recv, device):
        return pltpu.make_async_remote_copy(
            src_ref=src, dst_ref=dst, send_sem=send, recv_sem=recv,
            device_id=device, device_id_type=IDS)

    def copy_to(here, src, dst, send, recv, device):
        @pl.when(here)
        def _():
            pltpu.make_async_copy(src, dst, recv).start()

        @pl.when(jnp.logical_not(here))
        def _():
            remote(src, dst, send, recv, device).start()

    is_me = [(dp == d) & (rep == r) for d, r in OWNERS]
    owner = functools.reduce(jnp.logical_or, is_me)
    index = sum(b * m.astype(jnp.int32) for b, m in enumerate(is_me))

    barrier = pltpu.get_barrier_semaphore()

    @pl.when(owner)
    def _():
        for r in sorted(range(n_rep), key=lambda r: -min(r, n_rep - r)):
            for k in range(n_dp):
                if k or r:
                    pl.semaphore_signal(
                        barrier, inc=1, device_id=(lax.rem(dp + k, n_dp), lax.rem(rep + r, n_rep)),
                        device_id_type=IDS)

    state_hbm = (master_hbm, moment_hbm, second_hbm)
    loads = [pltpu.make_async_copy(ref, mine.at[i], load_sem.at[0]) for i, ref in enumerate(state_hbm)]
    for load in loads:
        load.start()
    with jax.named_scope("enter"):
        pl.semaphore_wait(barrier, n_own - owner.astype(jnp.int32))

    place = pl.ds(pl.multiple_of(dp * block, block), block)
    for b, device in enumerate(OWNERS):
        @pl.when(rep == b // per)
        def _():
            sub = b % per
            for i, ref in enumerate(state_hbm):
                copy_to(is_me[b], ref.at[sub * block:(sub + 1) * block], state_in.at[i, place],
                        send_sem.at[0], state_recv.at[0], device)

    slot = rep * n_dp + dp
    orders = {}
    for d in range(0, n_dp, 2):
        for r in range(n_rep):
            orders.setdefault(send_order((d, r)), []).append((dp // 2 == d // 2) & (rep == r))
    for order, places in orders.items():
        @pl.when(functools.reduce(jnp.logical_or, places))
        def _():
            for b in order:
                copy_to(is_me[b], grad_hbm.at[:, b * wide:(b + 1) * wide], raw_in.at[slot],
                        send_sem.at[0], raw_recv.at[rep // (n_rep - 1)], OWNERS[b])

    lane = lax.broadcasted_iota(jnp.int32, (rows, LANES), 1)
    mat = lax.broadcasted_iota(jnp.int32, (rows, LANES), 0) // (rows // MATS)

    def squares(parts):
        total = sum(v * v for v in parts)
        spread = jnp.where(lane == mat, jnp.sum(total, axis=1, keepdims=True), 0.0)
        return jnp.broadcast_to(jnp.sum(spread, axis=0, keepdims=True), (rows, LANES))

    @pl.when(owner)
    def _():
        early = (n_rep - 1) * n_dp
        with jax.named_scope("wait_state"):
            settle(state_in, state_recv.at[0])
        state = [[state_in[i, pl.ds(t, rows, stride=block), :] for i in range(3)] for t in range(block)]
        msg_out[block + 1] = squares([master for master, _, _ in state])
        with jax.named_scope("wait_early"):
            settle(raw_in.at[0:early], raw_recv.at[0])
        total = raw_in[0].astype(f32)
        for s in range(1, early):
            total = total + raw_in[s].astype(f32)
        with jax.named_scope("wait_late"):
            settle(raw_in.at[early:], raw_recv.at[1])
        for s in range(early, n_dp * n_rep):
            total = total + raw_in[s].astype(f32)
        total = total * (1.0 / (n_dp * n_rep))
        moved = []
        for t, (master, moment, second) in enumerate(state):
            grad = total[:, t * LANES:(t + 1) * LANES]
            grad_out[t] = grad
            msg_out[t], _, _, direction = adam(grad, master, moment, second)
            moved.append(direction)
        msg_out[block] = squares(moved)
        home = index // per
        targets = [(r, z) for z in range(n_rep) for r in range(rows)]
        for n, (r, z) in enumerate(targets):
            if n == 2:
                for s in range(rows):
                    copy_to((dp == s) & (rep == home), grad_out.at[:, s], grad_in.at[lax.rem(index, per)],
                            send_sem.at[0], result_recv.at[0], (s, home))
            copy_to((dp == r) & (rep == z), msg_out.at[:, r], msg_in.at[index],
                    send_sem.at[0], result_recv.at[0], (r, z))

    settle(mine, load_sem.at[0])
    with jax.named_scope("wait_results"):
        settle_rows(per * block + n_own * (block + 2), result_recv.at[0])
    for i, value in enumerate(adam(grad_in[...].reshape(per * block, LANES), mine[0], mine[1], mine[2])):
        blocks_out[i] = value
    norms = jnp.zeros((2, LANES), f32)
    for b in range(n_own):
        row_out[b * block:(b + 1) * block] = msg_in[b, 0:block]
        norms = norms + msg_in[b, block:]
    norms = jnp.sqrt(norms)
    ratio_out[...] = norms[0:1] / (norms[1:2] + 1e-06)

    raw_rows = rows * wide * 2 // (LANES * 4)
    state_rows = 3 * block
    owned = (n_own - 1) * raw_rows + rows * block + (n_dp * n_rep - 1) * (block + 2)
    at_home = rep == index // per

    @pl.when(jnp.logical_not(owner))
    def _():
        settle_rows(n_own * raw_rows + per * state_rows, send_sem.at[0])

    @pl.when(owner & at_home)
    def _():
        settle_rows(owned + (per - 1) * state_rows - block, send_sem.at[0])

    @pl.when(owner & jnp.logical_not(at_home))
    def _():
        settle_rows(owned + per * state_rows, send_sem.at[0])


def direct(raw_rows, flat, n_dp, n_rep):
    rows, width = raw_rows.shape
    n_own = len(OWNERS)
    per = n_own // n_rep
    length, wide = width // LANES, width // n_own
    block = wide // LANES
    f32 = jnp.float32
    dma = pltpu.SemaphoreType.DMA
    count = n_own * rows * wide // 256 + (3 * per + rows) * block + n_dp * n_rep * (block + 2)
    return pl.pallas_call(
        functools.partial(direct_kernel, n_dp, n_rep),
        out_shape=[
            pltpu.VMEM((length, LANES), f32),
            pltpu.VMEM((4, per * block, LANES), f32),
            pltpu.VMEM((1, LANES), f32),
        ],
        in_specs=[pl.BlockSpec(memory_space=pl.ANY)] * 4,
        out_specs=[pl.BlockSpec(memory_space=pltpu.VMEM)] * 3,
        scratch_shapes=[
            pltpu.VMEM((3, per * block, LANES), f32),
            pltpu.VMEM((n_dp * n_rep, rows, wide), jnp.bfloat16),
            pltpu.VMEM((3, rows * block, LANES), f32),
            pltpu.VMEM((count, LANES), f32),
            pltpu.VMEM((block, rows, LANES), f32),
            pltpu.VMEM((per, block, LANES), f32),
            pltpu.VMEM((block + 2, rows, LANES), f32),
            pltpu.VMEM((n_own, block + 2, LANES), f32),
            dma((1,)), dma((1,)), dma((2,)), dma((1,)), dma((1,)),
        ],
        compiler_params=pltpu.CompilerParams(collective_id=0, has_side_effects=True),
    )(raw_rows, *flat)


def rows_kernel(n_dp, n_rep, grad_hbm, master_hbm, moment_hbm, second_hbm,
                row_out, blocks_out, ratio_out,
                raw, state, tiles, rows_out, rows_in, parts, full, stats,
                load_sem, state_send, state_recv, row_send, row_recv,
                part_send, part_recv, stat_send, stat_recv):
    dp = lax.axis_index("dp")
    rep = lax.axis_index("replica")
    rows, width = raw.shape
    length = width // LANES
    block = length // n_rep

    def dp_peer(k):
        return {"dp": lax.rem(dp + k, n_dp)}

    def rep_peer(k):
        return {"replica": lax.rem(rep + k, n_rep)}

    def remote(src, dst, send, recv, peer):
        return pltpu.make_async_remote_copy(
            src_ref=src, dst_ref=dst, send_sem=send, recv_sem=recv,
            device_id=peer, device_id_type=IDS)

    def settle(ref, sem):
        pltpu.make_async_copy(ref, ref, sem.at[0]).wait()

    own = pl.ds(pl.multiple_of(rep * block, block), block)
    offsets = sorted(range(1, n_dp), key=lambda k: abs(2 * k - n_dp))
    grad_load = pltpu.make_async_copy(grad_hbm, raw, load_sem.at[0])
    grad_load.start()

    barrier = pltpu.get_barrier_semaphore()
    for k in offsets:
        pl.semaphore_signal(barrier, inc=1, device_id=dp_peer(k), device_id_type=IDS)
    for k in range(1, n_rep):
        pl.semaphore_signal(barrier, inc=1, device_id=rep_peer(k), device_id_type=IDS)

    state_loads = [
        pltpu.make_async_copy(ref, state.at[i, own], load_sem.at[1 + i])
        for i, ref in enumerate((master_hbm, moment_hbm, second_hbm))
    ]
    for load in state_loads:
        load.start()
    grad_load.wait()
    for t in range(length):
        tile = raw[:, t * LANES:(t + 1) * LANES].astype(jnp.float32)
        tiles[t * rows:(t + 1) * rows, :] = tile
    for k in offsets:
        peer = lax.rem(dp + k, n_dp)
        rows_out[k] = tiles[pl.ds(peer, length, stride=rows), :].astype(jnp.bfloat16)
    for load in state_loads:
        load.wait()
    pl.semaphore_wait(barrier, n_dp + n_rep - 2)

    for k in offsets:
        copy = remote(rows_out.at[k], rows_in.at[k], row_send.at[0], row_recv.at[0], dp_peer(k))
        copy.start()
    for k in range(1, n_rep):
        copy = remote(state.at[:, own], state.at[:, own], state_send.at[0], state_recv.at[0], rep_peer(k))
        copy.start()

    total = tiles[pl.ds(dp, length, stride=rows), :]
    settle(rows_in.at[1:n_dp], row_recv)
    for k in offsets:
        total = total + rows_in[k].astype(jnp.float32)
    parts[rep] = total
    for k in range(1, n_rep):
        copy = remote(parts.at[rep], parts.at[rep], part_send.at[0], part_recv.at[0], rep_peer(k))
        copy.start()

    settle(state.at[:, 0:(n_rep - 1) * block], state_recv)
    master = state[0]
    stats[dp, 1:2] = jnp.sum(master * master, axis=0, keepdims=True)
    old_moment = 0.9 * state[1]
    old_second = 0.999 * state[2]
    settle(rows_out.at[1:n_dp], row_send)
    settle(state.at[:, 0:(n_rep - 1) * block], state_send)
    settle(parts.at[1:n_rep], part_recv)
    summed = parts[0]
    for r in range(1, n_rep):
        summed = summed + parts[r]
    grad = summed * (1.0 / (n_dp * n_rep))
    new_moment = old_moment + 0.1 * grad
    new_second = old_second + 0.001 * grad * grad
    direction = new_moment * FIRST_SCALE / (jnp.sqrt(new_second * SECOND_SCALE) + 1e-08)
    stats[dp, 0:1] = jnp.sum(direction * direction, axis=0, keepdims=True)
    for k in offsets:
        copy = remote(stats.at[dp], stats.at[dp], stat_send.at[0], stat_recv.at[0], dp_peer(k))
        copy.start()

    new_master = master - 0.0003 * (direction + 0.1 * master)
    row_out[...] = new_master
    for i, value in enumerate((new_master, new_moment, new_second, direction)):
        full[i] = value
    for i in range(4):
        blocks_out[i] = full[i, own]
    settle(parts.at[1:n_rep], part_send)

    settle(stats.at[1:n_dp], stat_recv)
    per_mat = rows // MATS
    lane = lax.broadcasted_iota(jnp.int32, (1, LANES), 1)
    ratios = jnp.zeros((1, LANES), jnp.float32)
    for m in range(MATS):
        pair = stats[m * per_mat]
        for r in range(1, per_mat):
            pair = pair + stats[m * per_mat + r]
        norms = jnp.sqrt(jnp.sum(pair, axis=1, keepdims=True))
        ratio = norms[0:1] / (norms[1:2] + 1e-06)
        ratios = jnp.where(lane == m, ratio, ratios)
    ratio_out[...] = ratios

    settle(stats.at[1:n_dp], stat_send)


def by_rows(raw_rows, flat, n_dp, n_rep):
    rows, width = raw_rows.shape
    block = flat[0].shape[0]
    length = width // LANES
    f32 = jnp.float32
    vmem = pl.BlockSpec(memory_space=pltpu.VMEM)
    dma = pltpu.SemaphoreType.DMA
    return pl.pallas_call(
        functools.partial(rows_kernel, n_dp, n_rep),
        out_shape=[
            pltpu.VMEM((length, LANES), f32),
            pltpu.VMEM((4, block, LANES), f32),
            pltpu.VMEM((1, LANES), f32),
        ],
        in_specs=[pl.BlockSpec(memory_space=pl.ANY)] * 4,
        out_specs=[vmem] * 3,
        scratch_shapes=[
            pltpu.VMEM((rows, width), jnp.bfloat16),
            pltpu.VMEM((3, length, LANES), f32),
            pltpu.VMEM((rows * length, LANES), f32),
            pltpu.VMEM((n_dp, length, LANES), jnp.bfloat16),
            pltpu.VMEM((n_dp, length, LANES), jnp.bfloat16),
            pltpu.VMEM((n_rep, length, LANES), f32),
            pltpu.VMEM((4, length, LANES), f32),
            pltpu.VMEM((n_dp, 2, LANES), f32),
            dma((4,)),
            *[dma((1,))] * 8,
        ],
        compiler_params=pltpu.CompilerParams(collective_id=0, has_side_effects=True),
    )(raw_rows, *flat)


def finish(row_ref, blocks_ref, ratio_ref, params_out, master_out, moment_out, second_out, dir_out, ratio_out):
    for t in range(row_ref.shape[0]):
        params_out[:, t * LANES:(t + 1) * LANES] = row_ref[t:t + 1, :].astype(jnp.bfloat16)
    for i, out in enumerate((master_out, moment_out, second_out, dir_out)):
        out[...] = blocks_ref[i]
    ratio_out[...] = ratio_ref[0, :MATS]


def local(gradient, master, moment, second):
    raw_rows = gradient[0, 0]
    rows, width = raw_rows.shape
    n_dp = lax.axis_size("dp")
    n_rep = lax.axis_size("replica")
    cols = master.shape[1]
    block = cols // LANES
    f32 = jnp.float32
    vmem = pl.BlockSpec(memory_space=pltpu.VMEM)
    flat = [a.reshape(block, LANES) for a in (master, moment, second)]
    own_width = width // len(OWNERS)
    gathered = n_dp * n_rep * rows * own_width * 2
    fits = gathered <= DIRECT_BYTES and len(OWNERS) % n_rep == 0 and own_width % (8 * LANES) == 0
    exists = all(d < n_dp and r < n_rep for d, r in OWNERS)
    step = direct if fits and exists and rows == n_dp else by_rows
    row, blocks, ratios = step(raw_rows, flat, n_dp, n_rep)
    row, blocks, ratios = (
        pltpu.with_memory_space_constraint(a, pltpu.VMEM) for a in (row, blocks, ratios))
    outs = pl.pallas_call(
        finish,
        out_shape=[jax.ShapeDtypeStruct((1, width), jnp.bfloat16)]
        + [jax.ShapeDtypeStruct((block, LANES), f32)] * 4
        + [jax.ShapeDtypeStruct((MATS,), f32)],
        in_specs=[vmem] * 3,
        out_specs=[vmem] * 6,
    )(row, blocks, ratios)
    new_params, new_master, new_moment, new_second, direction, ratios = outs
    new_blocks = [a.reshape(1, cols) for a in (new_master, new_moment, new_second, direction)]
    return (new_params, *new_blocks, ratios)


def solution(mesh):
    return jax.shard_map(
        local,
        mesh=mesh,
        in_specs=(
            P("replica", "dp", None, None),
            P("dp", "replica"),
            P("dp", "replica"),
            P("dp", "replica"),
        ),
        out_specs=(
            P("dp", None),
            P("dp", "replica"),
            P("dp", "replica"),
            P("dp", "replica"),
            P("dp", "replica"),
            P(),
        ),
        check_vma=False,
    )
```

```python
import functools

import jax
import jax.numpy as jnp
from jax import lax
from jax.experimental import pallas as pl
from jax.experimental.pallas import tpu as pltpu
from jax.sharding import PartitionSpec as P

MATS = 4
STEP = 2
LANES = 128
IDS = pl.DeviceIdType.MESH
FIRST_SCALE = 1.0 / (1.0 - 0.9**STEP)
SECOND_SCALE = 1.0 / (1.0 - 0.999**STEP)
OWNERS = ((1, 0), (3, 0), (1, 1), (3, 1), (1, 2), (5, 1), (3, 2), (5, 2))
LEAD = (1.1, 0.2, 0.2, 1.5, 0.4, 1.0, 0.6, 0.6)
DIRECT_BYTES = 16 * 2**20


def hops(a, b):
    (u, p), (v, q) = a, b
    return abs(u // 2 % 2 - v // 2 % 2) + abs(u // 4 - v // 4) + abs(p - q)


def send_order(place):
    ties = (7, 6, 3, 1, 5, 4, 2, 0)
    return tuple(sorted(range(len(OWNERS)), key=lambda b: (-hops(place, OWNERS[b]) - LEAD[b], ties.index(b))))


def adam(grad, master, moment, second):
    new_moment = 0.9 * moment + 0.1 * grad
    new_second = 0.999 * second + 0.001 * grad * grad
    direction = new_moment * FIRST_SCALE / (jnp.sqrt(new_second * SECOND_SCALE) + 1e-08)
    new_master = master - 0.0003 * (direction + 0.1 * master)
    return new_master, new_moment, new_second, direction


def direct_kernel(n_dp, n_rep, grad_hbm, master_hbm, moment_hbm, second_hbm,
                  row_out, blocks_out, ratio_out,
                  mine, raw_in, state_in, rows_of, grad_out, grad_in, msg_out, msg_first, msg_in,
                  load_sem, send_sem, raw_recv, state_recv, result_recv):
    dp = lax.axis_index("dp")
    rep = lax.axis_index("replica")
    n_own = len(OWNERS)
    per = n_own // n_rep
    rows, width = grad_hbm.shape
    wide = width // n_own
    block = wide // LANES
    f32 = jnp.float32

    def settle(ref, sem):
        pltpu.make_async_copy(ref, ref, sem).wait()

    def settle_rows(count, sem):
        settle(rows_of.at[0:count], sem)

    def remote(src, dst, send, recv, device):
        return pltpu.make_async_remote_copy(
            src_ref=src, dst_ref=dst, send_sem=send, recv_sem=recv,
            device_id=device, device_id_type=IDS)

    def copy_to(here, src, dst, send, recv, device):
        @pl.when(here)
        def _():
            pltpu.make_async_copy(src, dst, recv).start()

        @pl.when(jnp.logical_not(here))
        def _():
            remote(src, dst, send, recv, device).start()

    is_me = [(dp == d) & (rep == r) for d, r in OWNERS]
    owner = functools.reduce(jnp.logical_or, is_me)
    index = sum(b * m.astype(jnp.int32) for b, m in enumerate(is_me))

    barrier = pltpu.get_barrier_semaphore()

    @pl.when(owner)
    def _():
        for r in sorted(range(n_rep), key=lambda r: -min(r, n_rep - r)):
            for k in range(n_dp):
                if k or r:
                    pl.semaphore_signal(
                        barrier, inc=1, device_id=(lax.rem(dp + k, n_dp), lax.rem(rep + r, n_rep)),
                        device_id_type=IDS)

    state_hbm = (master_hbm, moment_hbm, second_hbm)
    loads = [pltpu.make_async_copy(ref, mine.at[i], load_sem.at[0]) for i, ref in enumerate(state_hbm)]
    for load in loads:
        load.start()
    with jax.named_scope("enter"):
        pl.semaphore_wait(barrier, n_own - owner.astype(jnp.int32))

    place = pl.ds(pl.multiple_of(dp * block, block), block)
    for b, device in enumerate(OWNERS):
        @pl.when(rep == b // per)
        def _():
            sub = b % per
            for i, ref in enumerate(state_hbm):
                copy_to(is_me[b], ref.at[sub * block:(sub + 1) * block], state_in.at[i, place],
                        send_sem.at[0], state_recv.at[0], device)

    slot = rep * n_dp + dp
    orders = {}
    for d in range(0, n_dp, 2):
        for r in range(n_rep):
            orders.setdefault(send_order((d, r)), []).append((dp // 2 == d // 2) & (rep == r))
    for order, places in orders.items():
        @pl.when(functools.reduce(jnp.logical_or, places))
        def _():
            for b in order:
                copy_to(is_me[b], grad_hbm.at[:, b * wide:(b + 1) * wide], raw_in.at[slot],
                        send_sem.at[0], raw_recv.at[rep // (n_rep - 1)], OWNERS[b])

    lane = lax.broadcasted_iota(jnp.int32, (rows, LANES), 1)
    mat = lax.broadcasted_iota(jnp.int32, (rows, LANES), 0) // (rows // MATS)

    def squares(parts):
        total = sum(v * v for v in parts)
        spread = jnp.where(lane == mat, jnp.sum(total, axis=1, keepdims=True), 0.0)
        return jnp.broadcast_to(jnp.sum(spread, axis=0, keepdims=True), (rows, LANES))

    @pl.when(owner)
    def _():
        early = (n_rep - 1) * n_dp
        with jax.named_scope("wait_state"):
            settle(state_in, state_recv.at[0])
        state = [[state_in[i, pl.ds(t, rows, stride=block), :] for i in range(3)] for t in range(block)]
        msg_out[block + 1] = squares([master for master, _, _ in state])
        with jax.named_scope("wait_early"):
            settle(raw_in.at[0:early], raw_recv.at[0])
        total = raw_in[0].astype(f32)
        for s in range(1, early):
            total = total + raw_in[s].astype(f32)
        with jax.named_scope("wait_late"):
            settle(raw_in.at[early:], raw_recv.at[1])
        for s in range(early, n_dp * n_rep):
            total = total + raw_in[s].astype(f32)
        total = total * (1.0 / (n_dp * n_rep))
        moved = []
        for t, (master, moment, second) in enumerate(state):
            grad = total[:, t * LANES:(t + 1) * LANES]
            grad_out[t] = grad
            msg_out[t], _, _, direction = adam(grad, master, moment, second)
            moved.append(direction)
        msg_out[block] = squares(moved)
        for r in range(2):
            for t in range(block + 2):
                msg_first[r, t:t + 1] = msg_out[t, r:r + 1]
        home = index // per
        targets = [(r, z) for z in range(n_rep) for r in range(rows)]
        for n, (r, z) in enumerate(targets):
            if n == 2:
                for s in range(rows):
                    copy_to((dp == s) & (rep == home), grad_out.at[:, s], grad_in.at[lax.rem(index, per)],
                            send_sem.at[0], result_recv.at[0], (s, home))
            copy_to((dp == r) & (rep == z), msg_first.at[r] if n < 2 else msg_out.at[:, r], msg_in.at[index],
                    send_sem.at[0], result_recv.at[0], (r, z))

    settle(mine, load_sem.at[0])
    with jax.named_scope("wait_results"):
        settle_rows(per * block + n_own * (block + 2), result_recv.at[0])
    for i, value in enumerate(adam(grad_in[...].reshape(per * block, LANES), mine[0], mine[1], mine[2])):
        blocks_out[i] = value
    norms = jnp.zeros((2, LANES), f32)
    for b in range(n_own):
        row_out[b * block:(b + 1) * block] = msg_in[b, 0:block]
        norms = norms + msg_in[b, block:]
    norms = jnp.sqrt(norms)
    ratio_out[...] = norms[0:1] / (norms[1:2] + 1e-06)

    raw_rows = rows * wide * 2 // (LANES * 4)
    state_rows = 3 * block
    owned = (n_own - 1) * raw_rows + rows * block + (n_dp * n_rep - 1) * (block + 2)
    at_home = rep == index // per

    @pl.when(jnp.logical_not(owner))
    def _():
        settle_rows(n_own * raw_rows + per * state_rows, send_sem.at[0])

    @pl.when(owner & at_home)
    def _():
        settle_rows(owned + (per - 1) * state_rows - block, send_sem.at[0])

    @pl.when(owner & jnp.logical_not(at_home))
    def _():
        settle_rows(owned + per * state_rows, send_sem.at[0])


def direct(raw_rows, flat, n_dp, n_rep):
    rows, width = raw_rows.shape
    n_own = len(OWNERS)
    per = n_own // n_rep
    length, wide = width // LANES, width // n_own
    block = wide // LANES
    f32 = jnp.float32
    dma = pltpu.SemaphoreType.DMA
    count = n_own * rows * wide // 256 + (3 * per + rows) * block + n_dp * n_rep * (block + 2)
    return pl.pallas_call(
        functools.partial(direct_kernel, n_dp, n_rep),
        out_shape=[
            pltpu.VMEM((length, LANES), f32),
            pltpu.VMEM((4, per * block, LANES), f32),
            pltpu.VMEM((1, LANES), f32),
        ],
        in_specs=[pl.BlockSpec(memory_space=pl.ANY)] * 4,
        out_specs=[pl.BlockSpec(memory_space=pltpu.VMEM)] * 3,
        scratch_shapes=[
            pltpu.VMEM((3, per * block, LANES), f32),
            pltpu.VMEM((n_dp * n_rep, rows, wide), jnp.bfloat16),
            pltpu.VMEM((3, rows * block, LANES), f32),
            pltpu.VMEM((count, LANES), f32),
            pltpu.VMEM((block, rows, LANES), f32),
            pltpu.VMEM((per, block, LANES), f32),
            pltpu.VMEM((block + 2, rows, LANES), f32),
            pltpu.VMEM((2, block + 2, LANES), f32),
            pltpu.VMEM((n_own, block + 2, LANES), f32),
            dma((1,)), dma((1,)), dma((2,)), dma((1,)), dma((1,)),
        ],
        compiler_params=pltpu.CompilerParams(collective_id=0, has_side_effects=True),
    )(raw_rows, *flat)


def rows_kernel(n_dp, n_rep, grad_hbm, master_hbm, moment_hbm, second_hbm,
                row_out, blocks_out, ratio_out,
                raw, state, tiles, rows_out, rows_in, parts, full, stats,
                load_sem, state_send, state_recv, row_send, row_recv,
                part_send, part_recv, stat_send, stat_recv):
    dp = lax.axis_index("dp")
    rep = lax.axis_index("replica")
    rows, width = raw.shape
    length = width // LANES
    block = length // n_rep

    def dp_peer(k):
        return {"dp": lax.rem(dp + k, n_dp)}

    def rep_peer(k):
        return {"replica": lax.rem(rep + k, n_rep)}

    def remote(src, dst, send, recv, peer):
        return pltpu.make_async_remote_copy(
            src_ref=src, dst_ref=dst, send_sem=send, recv_sem=recv,
            device_id=peer, device_id_type=IDS)

    def settle(ref, sem):
        pltpu.make_async_copy(ref, ref, sem.at[0]).wait()

    own = pl.ds(pl.multiple_of(rep * block, block), block)
    offsets = sorted(range(1, n_dp), key=lambda k: abs(2 * k - n_dp))
    grad_load = pltpu.make_async_copy(grad_hbm, raw, load_sem.at[0])
    grad_load.start()

    barrier = pltpu.get_barrier_semaphore()
    for k in offsets:
        pl.semaphore_signal(barrier, inc=1, device_id=dp_peer(k), device_id_type=IDS)
    for k in range(1, n_rep):
        pl.semaphore_signal(barrier, inc=1, device_id=rep_peer(k), device_id_type=IDS)

    state_loads = [
        pltpu.make_async_copy(ref, state.at[i, own], load_sem.at[1 + i])
        for i, ref in enumerate((master_hbm, moment_hbm, second_hbm))
    ]
    for load in state_loads:
        load.start()
    grad_load.wait()
    for t in range(length):
        tile = raw[:, t * LANES:(t + 1) * LANES].astype(jnp.float32)
        tiles[t * rows:(t + 1) * rows, :] = tile
    for k in offsets:
        peer = lax.rem(dp + k, n_dp)
        rows_out[k] = tiles[pl.ds(peer, length, stride=rows), :].astype(jnp.bfloat16)
    for load in state_loads:
        load.wait()
    pl.semaphore_wait(barrier, n_dp + n_rep - 2)

    for k in offsets:
        copy = remote(rows_out.at[k], rows_in.at[k], row_send.at[0], row_recv.at[0], dp_peer(k))
        copy.start()
    for k in range(1, n_rep):
        copy = remote(state.at[:, own], state.at[:, own], state_send.at[0], state_recv.at[0], rep_peer(k))
        copy.start()

    total = tiles[pl.ds(dp, length, stride=rows), :]
    settle(rows_in.at[1:n_dp], row_recv)
    for k in offsets:
        total = total + rows_in[k].astype(jnp.float32)
    parts[rep] = total
    for k in range(1, n_rep):
        copy = remote(parts.at[rep], parts.at[rep], part_send.at[0], part_recv.at[0], rep_peer(k))
        copy.start()

    settle(state.at[:, 0:(n_rep - 1) * block], state_recv)
    master = state[0]
    stats[dp, 1:2] = jnp.sum(master * master, axis=0, keepdims=True)
    old_moment = 0.9 * state[1]
    old_second = 0.999 * state[2]
    settle(rows_out.at[1:n_dp], row_send)
    settle(state.at[:, 0:(n_rep - 1) * block], state_send)
    settle(parts.at[1:n_rep], part_recv)
    summed = parts[0]
    for r in range(1, n_rep):
        summed = summed + parts[r]
    grad = summed * (1.0 / (n_dp * n_rep))
    new_moment = old_moment + 0.1 * grad
    new_second = old_second + 0.001 * grad * grad
    direction = new_moment * FIRST_SCALE / (jnp.sqrt(new_second * SECOND_SCALE) + 1e-08)
    stats[dp, 0:1] = jnp.sum(direction * direction, axis=0, keepdims=True)
    for k in offsets:
        copy = remote(stats.at[dp], stats.at[dp], stat_send.at[0], stat_recv.at[0], dp_peer(k))
        copy.start()

    new_master = master - 0.0003 * (direction + 0.1 * master)
    row_out[...] = new_master
    for i, value in enumerate((new_master, new_moment, new_second, direction)):
        full[i] = value
    for i in range(4):
        blocks_out[i] = full[i, own]
    settle(parts.at[1:n_rep], part_send)

    settle(stats.at[1:n_dp], stat_recv)
    per_mat = rows // MATS
    lane = lax.broadcasted_iota(jnp.int32, (1, LANES), 1)
    ratios = jnp.zeros((1, LANES), jnp.float32)
    for m in range(MATS):
        pair = stats[m * per_mat]
        for r in range(1, per_mat):
            pair = pair + stats[m * per_mat + r]
        norms = jnp.sqrt(jnp.sum(pair, axis=1, keepdims=True))
        ratio = norms[0:1] / (norms[1:2] + 1e-06)
        ratios = jnp.where(lane == m, ratio, ratios)
    ratio_out[...] = ratios

    settle(stats.at[1:n_dp], stat_send)


def by_rows(raw_rows, flat, n_dp, n_rep):
    rows, width = raw_rows.shape
    block = flat[0].shape[0]
    length = width // LANES
    f32 = jnp.float32
    vmem = pl.BlockSpec(memory_space=pltpu.VMEM)
    dma = pltpu.SemaphoreType.DMA
    return pl.pallas_call(
        functools.partial(rows_kernel, n_dp, n_rep),
        out_shape=[
            pltpu.VMEM((length, LANES), f32),
            pltpu.VMEM((4, block, LANES), f32),
            pltpu.VMEM((1, LANES), f32),
        ],
        in_specs=[pl.BlockSpec(memory_space=pl.ANY)] * 4,
        out_specs=[vmem] * 3,
        scratch_shapes=[
            pltpu.VMEM((rows, width), jnp.bfloat16),
            pltpu.VMEM((3, length, LANES), f32),
            pltpu.VMEM((rows * length, LANES), f32),
            pltpu.VMEM((n_dp, length, LANES), jnp.bfloat16),
            pltpu.VMEM((n_dp, length, LANES), jnp.bfloat16),
            pltpu.VMEM((n_rep, length, LANES), f32),
            pltpu.VMEM((4, length, LANES), f32),
            pltpu.VMEM((n_dp, 2, LANES), f32),
            dma((4,)),
            *[dma((1,))] * 8,
        ],
        compiler_params=pltpu.CompilerParams(collective_id=0, has_side_effects=True),
    )(raw_rows, *flat)


def finish(row_ref, blocks_ref, ratio_ref, params_out, master_out, moment_out, second_out, dir_out, ratio_out):
    for t in range(row_ref.shape[0]):
        params_out[:, t * LANES:(t + 1) * LANES] = row_ref[t:t + 1, :].astype(jnp.bfloat16)
    for i, out in enumerate((master_out, moment_out, second_out, dir_out)):
        out[...] = blocks_ref[i]
    ratio_out[...] = ratio_ref[0, :MATS]


def local(gradient, master, moment, second):
    raw_rows = gradient[0, 0]
    rows, width = raw_rows.shape
    n_dp = lax.axis_size("dp")
    n_rep = lax.axis_size("replica")
    cols = master.shape[1]
    block = cols // LANES
    f32 = jnp.float32
    vmem = pl.BlockSpec(memory_space=pltpu.VMEM)
    flat = [a.reshape(block, LANES) for a in (master, moment, second)]
    own_width = width // len(OWNERS)
    gathered = n_dp * n_rep * rows * own_width * 2
    fits = gathered <= DIRECT_BYTES and len(OWNERS) % n_rep == 0 and own_width % (8 * LANES) == 0
    exists = all(d < n_dp and r < n_rep for d, r in OWNERS)
    step = direct if fits and exists and rows == n_dp else by_rows
    row, blocks, ratios = step(raw_rows, flat, n_dp, n_rep)
    row, blocks, ratios = (
        pltpu.with_memory_space_constraint(a, pltpu.VMEM) for a in (row, blocks, ratios))
    outs = pl.pallas_call(
        finish,
        out_shape=[jax.ShapeDtypeStruct((1, width), jnp.bfloat16)]
        + [jax.ShapeDtypeStruct((block, LANES), f32)] * 4
        + [jax.ShapeDtypeStruct((MATS,), f32)],
        in_specs=[vmem] * 3,
        out_specs=[vmem] * 6,
    )(row, blocks, ratios)
    new_params, new_master, new_moment, new_second, direction, ratios = outs
    new_blocks = [a.reshape(1, cols) for a in (new_master, new_moment, new_second, direction)]
    return (new_params, *new_blocks, ratios)


def solution(mesh):
    return jax.shard_map(
        local,
        mesh=mesh,
        in_specs=(
            P("replica", "dp", None, None),
            P("dp", "replica"),
            P("dp", "replica"),
            P("dp", "replica"),
        ),
        out_specs=(
            P("dp", None),
            P("dp", "replica"),
            P("dp", "replica"),
            P("dp", "replica"),
            P("dp", "replica"),
            P(),
        ),
        check_vma=False,
    )
```

```python
import functools

import jax
import jax.numpy as jnp
from jax import lax
from jax.experimental import pallas as pl
from jax.experimental.pallas import tpu as pltpu
from jax.sharding import PartitionSpec as P

MATS = 4
STEP = 2
LANES = 128
IDS = pl.DeviceIdType.MESH
FIRST_SCALE = 1.0 / (1.0 - 0.9**STEP)
SECOND_SCALE = 1.0 / (1.0 - 0.999**STEP)
OWNERS = ((1, 0), (3, 0), (1, 1), (3, 1), (1, 2), (5, 1), (3, 2), (5, 2))
LEAD = (1.1, 0.2, 0.2, 1.5, 0.4, 1.0, 0.6, 0.6)
DIRECT_BYTES = 16 * 2**20


def hops(a, b):
    (u, p), (v, q) = a, b
    return abs(u // 2 % 2 - v // 2 % 2) + abs(u // 4 - v // 4) + abs(p - q)


def send_order(place):
    ties = (7, 6, 3, 1, 5, 4, 2, 0)
    return tuple(sorted(range(len(OWNERS)), key=lambda b: (-hops(place, OWNERS[b]) - LEAD[b], ties.index(b))))


def adam(grad, master, moment, second):
    new_moment = 0.9 * moment + 0.1 * grad
    new_second = 0.999 * second + 0.001 * grad * grad
    direction = new_moment * FIRST_SCALE / (jnp.sqrt(new_second * SECOND_SCALE) + 1e-08)
    new_master = master - 0.0003 * (direction + 0.1 * master)
    return new_master, new_moment, new_second, direction


def direct_kernel(n_dp, n_rep, grad_hbm, master_hbm, moment_hbm, second_hbm,
                  row_out, blocks_out, ratio_out,
                  mine, raw_in, state_in, rows_of, grad_out, grad_in, msg_out, msg_first, msg_in,
                  load_sem, send_sem, raw_recv, state_recv, result_recv):
    dp = lax.axis_index("dp")
    rep = lax.axis_index("replica")
    n_own = len(OWNERS)
    per = n_own // n_rep
    rows, width = grad_hbm.shape
    wide = width // n_own
    block = wide // LANES
    f32 = jnp.float32

    def settle(ref, sem):
        pltpu.make_async_copy(ref, ref, sem).wait()

    def settle_rows(count, sem):
        settle(rows_of.at[0:count], sem)

    def remote(src, dst, send, recv, device):
        return pltpu.make_async_remote_copy(
            src_ref=src, dst_ref=dst, send_sem=send, recv_sem=recv,
            device_id=device, device_id_type=IDS)

    def copy_to(here, src, dst, send, recv, device):
        @pl.when(here)
        def _():
            pltpu.make_async_copy(src, dst, recv).start()

        @pl.when(jnp.logical_not(here))
        def _():
            remote(src, dst, send, recv, device).start()

    is_me = [(dp == d) & (rep == r) for d, r in OWNERS]
    owner = functools.reduce(jnp.logical_or, is_me)
    index = sum(b * m.astype(jnp.int32) for b, m in enumerate(is_me))

    barrier = pltpu.get_barrier_semaphore()

    @pl.when(owner)
    def _():
        for r in sorted(range(n_rep), key=lambda r: -min(r, n_rep - r)):
            for k in range(n_dp):
                if k or r:
                    pl.semaphore_signal(
                        barrier, inc=1, device_id=(lax.rem(dp + k, n_dp), lax.rem(rep + r, n_rep)),
                        device_id_type=IDS)

    state_hbm = (master_hbm, moment_hbm, second_hbm)
    loads = [pltpu.make_async_copy(ref, mine.at[i], load_sem.at[0]) for i, ref in enumerate(state_hbm)]
    for load in loads:
        load.start()
    with jax.named_scope("enter"):
        pl.semaphore_wait(barrier, n_own - owner.astype(jnp.int32))

    place = pl.ds(pl.multiple_of(dp * block, block), block)
    for b, device in enumerate(OWNERS):
        @pl.when(rep == b // per)
        def _():
            sub = b % per
            for i, ref in enumerate(state_hbm):
                copy_to(is_me[b], ref.at[sub * block:(sub + 1) * block], state_in.at[i, place],
                        send_sem.at[0], state_recv.at[0], device)

    slot = rep * n_dp + dp
    orders = {}
    for d in range(0, n_dp, 2):
        for r in range(n_rep):
            orders.setdefault(send_order((d, r)), []).append((dp // 2 == d // 2) & (rep == r))
    for order, places in orders.items():
        @pl.when(functools.reduce(jnp.logical_or, places))
        def _():
            for b in order:
                copy_to(is_me[b], grad_hbm.at[:, b * wide:(b + 1) * wide], raw_in.at[slot],
                        send_sem.at[0], raw_recv.at[rep // (n_rep - 1)], OWNERS[b])

    lane = lax.broadcasted_iota(jnp.int32, (rows, LANES), 1)
    mat = lax.broadcasted_iota(jnp.int32, (rows, LANES), 0) // (rows // MATS)

    def squares(parts):
        total = sum(v * v for v in parts)
        spread = jnp.where(lane == mat, jnp.sum(total, axis=1, keepdims=True), 0.0)
        return jnp.broadcast_to(jnp.sum(spread, axis=0, keepdims=True), (rows, LANES))

    @pl.when(owner)
    def _():
        early = (n_rep - 1) * n_dp
        with jax.named_scope("wait_state"):
            settle(state_in, state_recv.at[0])
        state = [[state_in[i, pl.ds(t, rows, stride=block), :] for i in range(3)] for t in range(block)]
        weights = squares([master for master, _, _ in state])
        msg_out[block + 1] = weights
        for r in range(2):
            msg_first[r, block + 1:] = weights[r:r + 1]
        with jax.named_scope("wait_early"):
            settle(raw_in.at[0:early], raw_recv.at[0])
        total = raw_in[0].astype(f32)
        for s in range(1, early):
            total = total + raw_in[s].astype(f32)
        with jax.named_scope("wait_late"):
            settle(raw_in.at[early:], raw_recv.at[1])
        for s in range(early, n_dp * n_rep):
            total = total + raw_in[s].astype(f32)
        total = total * (1.0 / (n_dp * n_rep))
        moved = []
        for t, (master, moment, second) in enumerate(state):
            grad = total[:, t * LANES:(t + 1) * LANES]
            grad_out[t] = grad
            new_master, _, _, direction = adam(grad, master, moment, second)
            moved.append(direction)
            msg_out[t] = new_master
            for r in range(2):
                msg_first[r, t:t + 1] = new_master[r:r + 1]
        norms = squares(moved)
        msg_out[block] = norms
        for r in range(2):
            msg_first[r, block:block + 1] = norms[r:r + 1]
        home = index // per
        targets = [(r, z) for z in range(n_rep) for r in range(rows)]
        for n, (r, z) in enumerate(targets):
            if n == 2:
                for s in range(rows):
                    copy_to((dp == s) & (rep == home), grad_out.at[:, s], grad_in.at[lax.rem(index, per)],
                            send_sem.at[0], result_recv.at[0], (s, home))
            copy_to((dp == r) & (rep == z), msg_first.at[r] if n < 2 else msg_out.at[:, r], msg_in.at[index],
                    send_sem.at[0], result_recv.at[0], (r, z))

    settle(mine, load_sem.at[0])
    with jax.named_scope("wait_results"):
        settle_rows(per * block + n_own * (block + 2), result_recv.at[0])
    for i, value in enumerate(adam(grad_in[...].reshape(per * block, LANES), mine[0], mine[1], mine[2])):
        blocks_out[i] = value
    norms = jnp.zeros((2, LANES), f32)
    for b in range(n_own):
        row_out[b * block:(b + 1) * block] = msg_in[b, 0:block]
        norms = norms + msg_in[b, block:]
    norms = jnp.sqrt(norms)
    ratio_out[...] = norms[0:1] / (norms[1:2] + 1e-06)

    raw_rows = rows * wide * 2 // (LANES * 4)
    state_rows = 3 * block
    owned = (n_own - 1) * raw_rows + rows * block + (n_dp * n_rep - 1) * (block + 2)
    at_home = rep == index // per

    @pl.when(jnp.logical_not(owner))
    def _():
        settle_rows(n_own * raw_rows + per * state_rows, send_sem.at[0])

    @pl.when(owner & at_home)
    def _():
        settle_rows(owned + (per - 1) * state_rows - block, send_sem.at[0])

    @pl.when(owner & jnp.logical_not(at_home))
    def _():
        settle_rows(owned + per * state_rows, send_sem.at[0])


def direct(raw_rows, flat, n_dp, n_rep):
    rows, width = raw_rows.shape
    n_own = len(OWNERS)
    per = n_own // n_rep
    length, wide = width // LANES, width // n_own
    block = wide // LANES
    f32 = jnp.float32
    dma = pltpu.SemaphoreType.DMA
    count = n_own * rows * wide // 256 + (3 * per + rows) * block + n_dp * n_rep * (block + 2)
    return pl.pallas_call(
        functools.partial(direct_kernel, n_dp, n_rep),
        out_shape=[
            pltpu.VMEM((length, LANES), f32),
            pltpu.VMEM((4, per * block, LANES), f32),
            pltpu.VMEM((1, LANES), f32),
        ],
        in_specs=[pl.BlockSpec(memory_space=pl.ANY)] * 4,
        out_specs=[pl.BlockSpec(memory_space=pltpu.VMEM)] * 3,
        scratch_shapes=[
            pltpu.VMEM((3, per * block, LANES), f32),
            pltpu.VMEM((n_dp * n_rep, rows, wide), jnp.bfloat16),
            pltpu.VMEM((3, rows * block, LANES), f32),
            pltpu.VMEM((count, LANES), f32),
            pltpu.VMEM((block, rows, LANES), f32),
            pltpu.VMEM((per, block, LANES), f32),
            pltpu.VMEM((block + 2, rows, LANES), f32),
            pltpu.VMEM((2, block + 2, LANES), f32),
            pltpu.VMEM((n_own, block + 2, LANES), f32),
            dma((1,)), dma((1,)), dma((2,)), dma((1,)), dma((1,)),
        ],
        compiler_params=pltpu.CompilerParams(collective_id=0, has_side_effects=True),
    )(raw_rows, *flat)


def rows_kernel(n_dp, n_rep, grad_hbm, master_hbm, moment_hbm, second_hbm,
                row_out, blocks_out, ratio_out,
                raw, state, tiles, rows_out, rows_in, parts, full, stats,
                load_sem, state_send, state_recv, row_send, row_recv,
                part_send, part_recv, stat_send, stat_recv):
    dp = lax.axis_index("dp")
    rep = lax.axis_index("replica")
    rows, width = raw.shape
    length = width // LANES
    block = length // n_rep

    def dp_peer(k):
        return {"dp": lax.rem(dp + k, n_dp)}

    def rep_peer(k):
        return {"replica": lax.rem(rep + k, n_rep)}

    def remote(src, dst, send, recv, peer):
        return pltpu.make_async_remote_copy(
            src_ref=src, dst_ref=dst, send_sem=send, recv_sem=recv,
            device_id=peer, device_id_type=IDS)

    def settle(ref, sem):
        pltpu.make_async_copy(ref, ref, sem.at[0]).wait()

    own = pl.ds(pl.multiple_of(rep * block, block), block)
    offsets = sorted(range(1, n_dp), key=lambda k: abs(2 * k - n_dp))
    grad_load = pltpu.make_async_copy(grad_hbm, raw, load_sem.at[0])
    grad_load.start()

    barrier = pltpu.get_barrier_semaphore()
    for k in offsets:
        pl.semaphore_signal(barrier, inc=1, device_id=dp_peer(k), device_id_type=IDS)
    for k in range(1, n_rep):
        pl.semaphore_signal(barrier, inc=1, device_id=rep_peer(k), device_id_type=IDS)

    state_loads = [
        pltpu.make_async_copy(ref, state.at[i, own], load_sem.at[1 + i])
        for i, ref in enumerate((master_hbm, moment_hbm, second_hbm))
    ]
    for load in state_loads:
        load.start()
    grad_load.wait()
    for t in range(length):
        tile = raw[:, t * LANES:(t + 1) * LANES].astype(jnp.float32)
        tiles[t * rows:(t + 1) * rows, :] = tile
    for k in offsets:
        peer = lax.rem(dp + k, n_dp)
        rows_out[k] = tiles[pl.ds(peer, length, stride=rows), :].astype(jnp.bfloat16)
    for load in state_loads:
        load.wait()
    pl.semaphore_wait(barrier, n_dp + n_rep - 2)

    for k in offsets:
        copy = remote(rows_out.at[k], rows_in.at[k], row_send.at[0], row_recv.at[0], dp_peer(k))
        copy.start()
    for k in range(1, n_rep):
        copy = remote(state.at[:, own], state.at[:, own], state_send.at[0], state_recv.at[0], rep_peer(k))
        copy.start()

    total = tiles[pl.ds(dp, length, stride=rows), :]
    settle(rows_in.at[1:n_dp], row_recv)
    for k in offsets:
        total = total + rows_in[k].astype(jnp.float32)
    parts[rep] = total
    for k in range(1, n_rep):
        copy = remote(parts.at[rep], parts.at[rep], part_send.at[0], part_recv.at[0], rep_peer(k))
        copy.start()

    settle(state.at[:, 0:(n_rep - 1) * block], state_recv)
    master = state[0]
    stats[dp, 1:2] = jnp.sum(master * master, axis=0, keepdims=True)
    old_moment = 0.9 * state[1]
    old_second = 0.999 * state[2]
    settle(rows_out.at[1:n_dp], row_send)
    settle(state.at[:, 0:(n_rep - 1) * block], state_send)
    settle(parts.at[1:n_rep], part_recv)
    summed = parts[0]
    for r in range(1, n_rep):
        summed = summed + parts[r]
    grad = summed * (1.0 / (n_dp * n_rep))
    new_moment = old_moment + 0.1 * grad
    new_second = old_second + 0.001 * grad * grad
    direction = new_moment * FIRST_SCALE / (jnp.sqrt(new_second * SECOND_SCALE) + 1e-08)
    stats[dp, 0:1] = jnp.sum(direction * direction, axis=0, keepdims=True)
    for k in offsets:
        copy = remote(stats.at[dp], stats.at[dp], stat_send.at[0], stat_recv.at[0], dp_peer(k))
        copy.start()

    new_master = master - 0.0003 * (direction + 0.1 * master)
    row_out[...] = new_master
    for i, value in enumerate((new_master, new_moment, new_second, direction)):
        full[i] = value
    for i in range(4):
        blocks_out[i] = full[i, own]
    settle(parts.at[1:n_rep], part_send)

    settle(stats.at[1:n_dp], stat_recv)
    per_mat = rows // MATS
    lane = lax.broadcasted_iota(jnp.int32, (1, LANES), 1)
    ratios = jnp.zeros((1, LANES), jnp.float32)
    for m in range(MATS):
        pair = stats[m * per_mat]
        for r in range(1, per_mat):
            pair = pair + stats[m * per_mat + r]
        norms = jnp.sqrt(jnp.sum(pair, axis=1, keepdims=True))
        ratio = norms[0:1] / (norms[1:2] + 1e-06)
        ratios = jnp.where(lane == m, ratio, ratios)
    ratio_out[...] = ratios

    settle(stats.at[1:n_dp], stat_send)


def by_rows(raw_rows, flat, n_dp, n_rep):
    rows, width = raw_rows.shape
    block = flat[0].shape[0]
    length = width // LANES
    f32 = jnp.float32
    vmem = pl.BlockSpec(memory_space=pltpu.VMEM)
    dma = pltpu.SemaphoreType.DMA
    return pl.pallas_call(
        functools.partial(rows_kernel, n_dp, n_rep),
        out_shape=[
            pltpu.VMEM((length, LANES), f32),
            pltpu.VMEM((4, block, LANES), f32),
            pltpu.VMEM((1, LANES), f32),
        ],
        in_specs=[pl.BlockSpec(memory_space=pl.ANY)] * 4,
        out_specs=[vmem] * 3,
        scratch_shapes=[
            pltpu.VMEM((rows, width), jnp.bfloat16),
            pltpu.VMEM((3, length, LANES), f32),
            pltpu.VMEM((rows * length, LANES), f32),
            pltpu.VMEM((n_dp, length, LANES), jnp.bfloat16),
            pltpu.VMEM((n_dp, length, LANES), jnp.bfloat16),
            pltpu.VMEM((n_rep, length, LANES), f32),
            pltpu.VMEM((4, length, LANES), f32),
            pltpu.VMEM((n_dp, 2, LANES), f32),
            dma((4,)),
            *[dma((1,))] * 8,
        ],
        compiler_params=pltpu.CompilerParams(collective_id=0, has_side_effects=True),
    )(raw_rows, *flat)


def finish(row_ref, blocks_ref, ratio_ref, params_out, master_out, moment_out, second_out, dir_out, ratio_out):
    for t in range(row_ref.shape[0]):
        params_out[:, t * LANES:(t + 1) * LANES] = row_ref[t:t + 1, :].astype(jnp.bfloat16)
    for i, out in enumerate((master_out, moment_out, second_out, dir_out)):
        out[...] = blocks_ref[i]
    ratio_out[...] = ratio_ref[0, :MATS]


def local(gradient, master, moment, second):
    raw_rows = gradient[0, 0]
    rows, width = raw_rows.shape
    n_dp = lax.axis_size("dp")
    n_rep = lax.axis_size("replica")
    cols = master.shape[1]
    block = cols // LANES
    f32 = jnp.float32
    vmem = pl.BlockSpec(memory_space=pltpu.VMEM)
    flat = [a.reshape(block, LANES) for a in (master, moment, second)]
    own_width = width // len(OWNERS)
    gathered = n_dp * n_rep * rows * own_width * 2
    fits = gathered <= DIRECT_BYTES and len(OWNERS) % n_rep == 0 and own_width % (8 * LANES) == 0
    exists = all(d < n_dp and r < n_rep for d, r in OWNERS)
    step = direct if fits and exists and rows == n_dp else by_rows
    row, blocks, ratios = step(raw_rows, flat, n_dp, n_rep)
    row, blocks, ratios = (
        pltpu.with_memory_space_constraint(a, pltpu.VMEM) for a in (row, blocks, ratios))
    outs = pl.pallas_call(
        finish,
        out_shape=[jax.ShapeDtypeStruct((1, width), jnp.bfloat16)]
        + [jax.ShapeDtypeStruct((block, LANES), f32)] * 4
        + [jax.ShapeDtypeStruct((MATS,), f32)],
        in_specs=[vmem] * 3,
        out_specs=[vmem] * 6,
    )(row, blocks, ratios)
    new_params, new_master, new_moment, new_second, direction, ratios = outs
    new_blocks = [a.reshape(1, cols) for a in (new_master, new_moment, new_second, direction)]
    return (new_params, *new_blocks, ratios)


def solution(mesh):
    return jax.shard_map(
        local,
        mesh=mesh,
        in_specs=(
            P("replica", "dp", None, None),
            P("dp", "replica"),
            P("dp", "replica"),
            P("dp", "replica"),
        ),
        out_specs=(
            P("dp", None),
            P("dp", "replica"),
            P("dp", "replica"),
            P("dp", "replica"),
            P("dp", "replica"),
            P(),
        ),
        check_vma=False,
    )
```
